128 devices in a mesh: pair: 8 (over x, y_lo), vtile: 16 (over z, y_hi, core).
Axes of the slice: x: 4, y: 4 (y_hi: 2, y_lo: 2; y = y_hi * 2 + y_lo), z: 4, core: 2. Of those that a mesh axis runs over, the one named last changes fastest.
Arguments:
- amplitudes: bfloat16 [128, 512, 512], P(('pair', 'vtile')), may hold values from -1.1953125 to 1.1953125
- factors: bfloat16 [512, 512, 2048], P('vtile', 'pair'), may hold values from -0.125 to 0.125
- pair_list: int32 [128, 2], P(('pair', 'vtile')), may hold values from 0 to 127
- window_offsets: int32 [2], replicated, may hold values from 0 to 511
- occupied_energy: float32 [128], replicated, may hold values from -3 to -0.5
- virtual_energy: float32 [512], replicated, may hold values from 0.5 to 4
Outputs:
- residual: float32 [128, 2, 512], P(('pair', 'vtile'))
- update: float32 [128, 2, 512], P(('pair', 'vtile'))
The draws below stay inside these ranges and needn't reach their ends.
All inputs are finite; a program needn't handle non-finite values.
Results may differ from the reference program's by a relative error of at most 0.0029.
Values may be sent and summed in bfloat16 or wider, within the bound.
No kernel may reach another device: no remote copies, remote signals or barrier semaphores. Data moves between devices by JAX's collectives and lax.ppermute only.
A program may use at most 128 MiB of HBM per device.

```python
import math
import jax
import jax.numpy as jnp
from jax import lax

OCC = 128
VIRT = 512
AUX = 2048
AWIN = 2
PAIRS = 128


def with_ends(entries, stream_key, low, largest):
    spot = [jax.random.randint(jax.random.fold_in(stream_key, axis), (), 0, length) for axis, length in enumerate(entries.shape)]
    widest = entries.shape.index(max(entries.shape))
    next_to = spot[:widest] + [(spot[widest] + 1) % entries.shape[widest]] + spot[widest + 1:]
    return entries.at[tuple(spot)].set(low).at[tuple(next_to)].set(largest)


def shard_levels(own_key, dims, cuts, least, top_value):
    factor_of = 1.0
    for position, parts in cuts:
        heights = jax.random.uniform(jax.random.fold_in(jax.random.fold_in(own_key, 6), position), (parts,), jnp.float32, least / len(cuts), top_value / len(cuts))
        factor_of = factor_of * jnp.repeat(jnp.exp(heights), dims[position] // parts).reshape((-1,) + (1,) * (len(dims) - 1 - position))
    return factor_of


def gaussian(own_key, dims, spread, reach, cuts=(), kind=jnp.bfloat16):
    factor_of = shard_levels(own_key, dims, cuts, -0.22, 0.18) if cuts else 1.0
    drawn = jax.random.normal(own_key, dims, jnp.float32) * spread * factor_of
    return jnp.minimum(jnp.maximum(drawn, -reach), reach).astype(kind)


def setup_inputs(seed: int = 0) -> dict:
    arg_keys = jax.random.split(jax.random.key(seed), 7)
    return {
        "amplitudes": gaussian(arg_keys[0], (PAIRS, VIRT, VIRT), 0.2, 1.1953125, ((0, 128),)),
        "factors": gaussian(arg_keys[1], (VIRT, VIRT, AUX), AUX ** -0.5, 0.125, ((0, 16), (1, 8))),
        "pair_list": with_ends(jax.random.randint(arg_keys[2], (PAIRS, 2), 0, OCC), jax.random.fold_in(arg_keys[2], 1), 0, OCC - 1).astype(jnp.int32),
        "window_offsets": jax.random.randint(arg_keys[3], (AWIN,), 0, VIRT).astype(jnp.int32),
        "occupied_energy": jnp.clip(jax.random.uniform(arg_keys[4], (OCC,), jnp.float32, -3.0, -0.5), -3.0, -0.5),
        "virtual_energy": jnp.clip(jnp.exp(jax.random.uniform(arg_keys[5], (VIRT,), jnp.float32, math.log(0.5), math.log(4.0))), 0.5, 4.0),
    }


def reference(amplitudes, factors, pair_list, window_offsets, occupied_energy, virtual_energy):
    width = min(64, VIRT)
    arows = factors[window_offsets]
    left_side = arows.reshape(AWIN * VIRT, AUX)

    def one_range(range_index):
        offset = (range_index * width).astype(jnp.int32)
        slab = lax.dynamic_slice_in_dim(factors, offset, width, 1)
        integrals = jnp.dot(left_side, slab.reshape(VIRT * width, AUX).T, preferred_element_type=jnp.float32).astype(jnp.bfloat16)
        integrals = integrals.reshape(AWIN, VIRT, VIRT, width).transpose(0, 2, 1, 3).reshape(AWIN * VIRT, VIRT * width)
        tau_slab = lax.dynamic_slice_in_dim(amplitudes, offset, width, 2).reshape(PAIRS, VIRT * width)
        return jnp.dot(tau_slab, integrals.T, preferred_element_type=jnp.float32)

    pieces = lax.map(one_range, jnp.arange(VIRT // width, dtype=jnp.int32))
    residual = jnp.sum(pieces, axis=0).reshape(PAIRS, AWIN, VIRT)
    occupied_sum = occupied_energy[pair_list[:, 0]] + occupied_energy[pair_list[:, 1]]
    window_energy = virtual_energy[window_offsets]
    denominator = window_energy[None, :, None] + virtual_energy[None, None, :] - occupied_sum[:, None, None]
    update = residual / denominator
    return residual, update
```

```python
import functools

import jax
import jax.numpy as jnp
from jax import lax
from jax.experimental import pallas as pl
from jax.experimental.pallas import tpu as pltpu
from jax.sharding import Mesh, PartitionSpec as P

PAIR = ("x", "yl")
TILE = ("z", "yh", "c")
DB = 8


def shift(x, axis, step, size):
    return lax.ppermute(x, axis, [(i, (i + step) % size) for i in range(size)])


def lookup(table, indices):
    positions = jnp.arange(table.shape[0], dtype=jnp.int32)
    return jnp.sum(jnp.where(positions[None, :] == indices[:, None], table[None, :], 0.0), axis=1)


def integrals_kernel(order, b_ref, *refs):
    pieces, out, rows, sem = refs[:-3], refs[-3], refs[-2], refs[-1]
    width = pieces[0].shape[0]

    def copy(n):
        return pltpu.make_async_copy(pieces[n], rows.at[order[n]], sem.at[n])

    @pl.when(pl.program_id(0) == 0)
    def _():
        for n in range(len(pieces)):
            copy(n).start()
        for n in range(len(pieces)):
            copy(n).wait()

    slab = b_ref[...].reshape(-1, b_ref.shape[-1])
    count = rows.shape[0] * width // 2
    for k in range(2):
        half = rows[k * (rows.shape[0] // 2):(k + 1) * (rows.shape[0] // 2)].reshape(count, rows.shape[-1])
        value = lax.dot_general(slab, half, (((1,), (1,)), ((), ())), preferred_element_type=jnp.float32)
        out[k * slab.shape[0]:(k + 1) * slab.shape[0], :] = value.astype(jnp.bfloat16)


def contract_kernel(order, integrals, *refs):
    pieces, out, held, sem = refs[:-3], refs[-3], refs[-2], refs[-1]
    depth = pieces[0].shape[0]
    group = 4

    def copy(n):
        return pltpu.make_async_copy(pieces[n], held.at[pl.ds(n * depth, depth), :], sem.at[n])

    for n in range(len(pieces)):
        copy(n).start()
    columns = integrals.shape[0]
    folds = columns // DB
    pick_r = lax.broadcasted_iota(jnp.int32, (columns, folds), 0) // DB
    pick_c = lax.broadcasted_iota(jnp.int32, (columns, folds), 1)
    fold = (pick_r == pick_c).astype(jnp.float32)
    size = group * depth
    row = lax.broadcasted_iota(jnp.int32, (size, columns), 0) % DB
    col = lax.broadcasted_iota(jnp.int32, (size, columns), 1) % DB
    same = row == col
    for g in range(len(pieces) // group):
        for n in range(g * group, (g + 1) * group):
            copy(n).wait()
        value = lax.dot_general(
            held[g * size:(g + 1) * size, :], integrals[...], (((1,), (1,)), ((), ())),
            preferred_element_type=jnp.float32)
        value = jnp.where(same, value, 0.0).reshape(size // DB, DB, columns).sum(axis=1)
        value = lax.dot_general(value, fold, (((1,), (0,)), ((), ())),
                                precision=lax.Precision.HIGHEST, preferred_element_type=jnp.float32)
        value = value.reshape(group, depth // DB, folds)
        for n in range(group):
            out[order[g * group + n]] = value[n]


def local(amplitudes, factors, pair_list, window_offsets, occupied_energy, virtual_energy):
    rows_here, cols_here, aux = factors.shape
    virt = amplitudes.shape[1]
    x, yl, z, yh, c = (lax.axis_index(a) for a in ("x", "yl", "z", "yh", "c"))

    tau = amplitudes[0].T.reshape(8, cols_here, virt)
    tau = lax.all_to_all(tau, PAIR, split_axis=0, concat_axis=0, tiled=True)
    tau = tau.reshape(8, cols_here // DB, DB, virt).transpose(0, 2, 1, 3).reshape(8 * DB, cols_here // DB * virt)
    tau_h = shift(tau, "yh", 1, 2)

    owner = window_offsets // rows_here
    row_of = window_offsets % rows_here
    mine = lax.dynamic_index_in_dim(factors, lax.dynamic_index_in_dim(row_of, c, 0, False), 0, False)
    other = lax.dynamic_index_in_dim(factors, lax.dynamic_index_in_dim(row_of, 1 - c, 0, False), 0, False)
    own = lax.dynamic_index_in_dim(owner, c, 0, False)
    own_z, own_h, own_c = own // 4, own // 2 % 2, own % 2
    swapped = shift(other, "c", 1, 2)
    arow = jnp.where(own_c == c, mine, swapped)
    half = arow.shape[0] // 2
    up = shift(arow, "z", 1, 4)
    down = shift(arow, "z", -1, 4)
    far = jnp.concatenate([shift(up[:half], "z", 1, 4), shift(down[half:], "z", -1, 4)])
    rel = (own_z - z) % 4
    arow = jnp.where(rel == 0, arow, jnp.where(rel == 3, up, jnp.where(rel == 1, down, far)))
    cross = shift(arow, "yh", 1, 2)
    arow = jnp.where(own_h == yh, arow, cross)
    arow_l = shift(arow, "yl", 1, 2)
    near = [arow, arow_l]
    up = [shift(a, "x", 1, 4) for a in near]
    down = [shift(a, "x", -1, 4) for a in near]
    far = [shift(up[0], "x", 1, 4), shift(down[1], "x", -1, 4)]
    blocks = near + up + down + far
    places = [(dx, dl) for dx in (0, 3, 1, 2) for dl in (0, 1)]
    blocks = blocks + [shift(a, "c", 1, 2) for a in blocks]
    row_order = jnp.stack([
        k * 8 + (x + dx) % 4 * 2 + (yl + dl) % 2 for k in (c, 1 - c) for dx, dl in places]).astype(jnp.int32)

    n_d = cols_here // DB
    any_spec = pl.BlockSpec(memory_space=pl.ANY)
    integrals = pl.pallas_call(
        integrals_kernel,
        out_shape=jax.ShapeDtypeStruct((2 * rows_here * DB, n_d * virt), jnp.bfloat16),
        grid_spec=pltpu.PrefetchScalarGridSpec(
            num_scalar_prefetch=1, grid=(n_d,),
            in_specs=[pl.BlockSpec((rows_here, DB, aux), lambda d, o: (0, d, 0))] + [any_spec] * 16,
            out_specs=pl.BlockSpec((2 * rows_here * DB, virt), lambda d, o: (0, d)),
            scratch_shapes=[pltpu.VMEM((16, cols_here, aux), jnp.bfloat16), pltpu.SemaphoreType.DMA((16,))]),
        compiler_params=pltpu.CompilerParams(vmem_limit_bytes=40 << 20),
        cost_estimate=pl.CostEstimate(flops=2 * 1024 * 2048 * 2048, bytes_accessed=16 << 20, transcendentals=0),
        name="integrals",
    )(row_order, factors, *blocks)

    near = [tau, tau_h]
    up = [shift(a, "z", 1, 4) for a in near]
    down = [shift(a, "z", -1, 4) for a in near]
    far = [shift(up[0], "z", 1, 4), shift(down[1], "z", -1, 4)]
    pieces = near + up + down + far
    where_z = [(0, 0), (0, 1), (3, 0), (3, 1), (1, 0), (1, 1), (2, 0), (2, 1)]
    pieces = pieces + [shift(a, "c", 1, 2) for a in pieces]
    tau_order = jnp.stack([
        (z + dz) % 4 * 4 + (yh + dh) % 2 * 2 + cc for cc in (c, 1 - c) for dz, dh in where_z]).astype(jnp.int32)

    partial = pl.pallas_call(
        contract_kernel,
        out_shape=jax.ShapeDtypeStruct((16, 8, 2 * rows_here), jnp.float32),
        grid_spec=pltpu.PrefetchScalarGridSpec(
            num_scalar_prefetch=1, grid=(1,),
            in_specs=[pl.BlockSpec(integrals.shape, lambda g, o: (0, 0))] + [any_spec] * 16,
            out_specs=pl.BlockSpec((16, 8, 2 * rows_here), lambda g, o: (0, 0, 0)),
            scratch_shapes=[pltpu.VMEM((1024, n_d * virt), jnp.bfloat16), pltpu.SemaphoreType.DMA((16,))]),
        compiler_params=pltpu.CompilerParams(vmem_limit_bytes=40 << 20),
        cost_estimate=pl.CostEstimate(flops=2 * 1024 * 512 * 4096, bytes_accessed=12 << 20, transcendentals=0),
        name="contract",
    )(tau_order, integrals, *pieces)

    parts = lax.all_to_all(partial.reshape(128, 2 * rows_here), TILE + PAIR, split_axis=0, concat_axis=0, tiled=True)
    residual = parts.reshape(16, 8, 2, rows_here).sum(axis=1).transpose(1, 0, 2).reshape(1, 2, 16 * rows_here)
    occupied_sum = lookup(occupied_energy, pair_list[:, 0]) + lookup(occupied_energy, pair_list[:, 1])
    window_energy = lookup(virtual_energy, window_offsets)
    denominator = (
        window_energy[None, :, None] + virtual_energy[None, None, :] - occupied_sum[:, None, None]
    )
    return residual, residual / denominator


def solution(mesh):
    fine = Mesh(mesh.devices.reshape(4, 2, 4, 2, 2), PAIR + TILE)
    return jax.shard_map(
        local,
        mesh=fine,
        in_specs=(P(PAIR + TILE, None, None), P(TILE, PAIR, None), P(PAIR + TILE, None), P(), P(), P()),
        out_specs=(P(PAIR + TILE, None, None), P(PAIR + TILE, None, None)),
        check_vma=False,
    )
```

```python
import functools

import jax
import jax.numpy as jnp
from jax import lax
from jax.experimental import pallas as pl
from jax.experimental.pallas import tpu as pltpu
from jax.sharding import Mesh, PartitionSpec as P

PAIR = ("x", "yl")
TILE = ("z", "yh", "c")
DB = 8
LANES = 128


def shift(x, axis, step, size):
    return lax.ppermute(x, axis, [(i, (i + step) % size) for i in range(size)])


def shift_y(x, step):
    at = [y % 2 * 2 + y // 2 for y in range(4)]
    return lax.ppermute(x, ("yl", "yh"), [(at[y], at[(y + step) % 4]) for y in range(4)])


def lookup(table, indices):
    positions = jnp.arange(table.shape[0], dtype=jnp.int32)
    return jnp.sum(jnp.where(positions[None, :] == indices[:, None], table[None, :], 0.0), axis=1)


def pick_kernel(rows, offsets, factors, mine, other, sem):
    c = lax.axis_index("c")
    first = pltpu.make_async_copy(factors.at[offsets[c] % rows], mine, sem.at[0])
    second = pltpu.make_async_copy(factors.at[offsets[1 - c] % rows], other, sem.at[1])
    first.start()
    second.start()
    first.wait()
    second.wait()


def halve_kernel(rows, offsets, mine, swapped, keep, send, sem):
    c, h = lax.axis_index("c"), lax.axis_index("yh")
    size = keep.shape[0]

    def move(source):
        first = pltpu.make_async_copy(source.at[pl.ds(h * size, size), :], keep, sem.at[0])
        second = pltpu.make_async_copy(source.at[pl.ds((1 - h) * size, size), :], send, sem.at[1])
        first.start()
        second.start()
        first.wait()
        second.wait()

    here = offsets[c] // rows % 2 == c

    @pl.when(here)
    def _():
        move(mine)

    @pl.when(jnp.logical_not(here))
    def _():
        move(swapped)


def choose_kernel(rows, offsets, keep, got, out, sem):
    here = offsets[lax.axis_index("c")] // (2 * rows) % 2 == lax.axis_index("yh")
    for source, wanted in ((keep, here), (got, jnp.logical_not(here))):
        @pl.when(wanted)
        def _():
            copy = pltpu.make_async_copy(source, out, sem.at[0])
            copy.start()
            copy.wait()


def choose_z_kernel(rows, offsets, own, up, down, far, out, sem):
    rel = (offsets[lax.axis_index("c")] // (4 * rows) + 4 - lax.axis_index("z")) % 4
    for source, wanted in ((own, 0), (down, 1), (far, 2), (up, 3)):
        @pl.when(rel == wanted)
        def _():
            copy = pltpu.make_async_copy(source, out, sem.at[0])
            copy.start()
            copy.wait()


def place_kernel(own, up, down, far, out, sem):
    y = lax.axis_index("yh") * 2 + lax.axis_index("yl")
    size = own.shape[0]
    copies = []
    for n, (piece, step) in enumerate(((own, 0), (up, 3), (down, 1), (far, 2))):
        at = (y + step) % 4
        at = at % 2 * 2 + at // 2
        copies.append(pltpu.make_async_copy(piece, out.at[pl.ds(at * size, size), :], sem.at[n]))
    for copy in copies:
        copy.start()
    for copy in copies:
        copy.wait()


ANY = pl.BlockSpec(memory_space=pl.ANY)
SMALL = pl.BlockSpec(memory_space=pltpu.SMEM)


def move_call(body, name, shapes, n_in, n_sem, small=True):
    specs = ([SMALL] if small else []) + [ANY] * n_in
    return pl.pallas_call(
        body,
        out_shape=[jax.ShapeDtypeStruct(shape, jnp.bfloat16) for shape in shapes],
        in_specs=specs,
        out_specs=[ANY] * len(shapes),
        scratch_shapes=[pltpu.SemaphoreType.DMA((n_sem,))],
        compiler_params=pltpu.CompilerParams(vmem_limit_bytes=1 << 20),
        cost_estimate=pl.CostEstimate(flops=0, bytes_accessed=1 << 20, transcendentals=0),
        name=name,
    )


def integrals(held, pieces, flips, out):
    rows, cols, aux = held.shape
    deep = 2 * DB
    side = [p[...] for p in pieces]
    side = jnp.concatenate(side, axis=0)
    for step in range(cols // deep):
        yield step
        slab = held[:, step * deep:(step + 1) * deep, :].reshape(rows * deep, aux)
        value = lax.dot_general(slab, side, (((1,), (1,)), ((), ())), preferred_element_type=jnp.float32)
        value = value.astype(jnp.bfloat16).reshape(rows, deep // DB, DB, side.shape[0])
        for n in range(side.shape[0] // LANES):
            k = (n + flips[n // 2]) % 2
            for d in range(deep // DB):
                block = value[:, d, :, n * LANES:(n + 1) * LANES].reshape(rows * DB, LANES)
                at = step * deep // DB + d
                out[n // 2, k * rows * DB:(k + 1) * rows * DB, at * LANES:(at + 1) * LANES] = block


def first_kernel(factors, first, second, out, held, sem):
    deep = 2 * DB
    copies = []
    for step in range(held.shape[1] // deep):
        part = pl.ds(step * deep, deep)
        copies.append(pltpu.make_async_copy(factors.at[:, part, :], held.at[:, part, :], sem.at[step]))
        copies[-1].start()
    for step in integrals(held, (first, second), (0,), out):
        copies[step].wait()


def next_kernel(flips, held, *refs):
    for _ in integrals(held, refs[:-1], flips, refs[-1]):
        pass


IN_VMEM = pl.BlockSpec(memory_space=pltpu.VMEM)
IN_HBM = pl.BlockSpec(memory_space=pltpu.HBM)


def integrals_of(factors, pieces, flips, name, load=False):
    rows, cols, aux = factors.shape
    count = len(flips)
    out_shape = [jax.ShapeDtypeStruct((count, 2 * rows * DB, cols // DB * LANES), jnp.bfloat16)]
    if load:
        out_shape.append(jax.ShapeDtypeStruct(factors.shape, factors.dtype))
    return pl.pallas_call(
        first_kernel if load else functools.partial(next_kernel, flips),
        out_shape=out_shape,
        in_specs=[IN_HBM if load else IN_VMEM] + [IN_VMEM] * len(pieces),
        out_specs=[IN_VMEM] * len(out_shape),
        scratch_shapes=[pltpu.SemaphoreType.DMA((4,))] if load else [],
        compiler_params=pltpu.CompilerParams(vmem_limit_bytes=12 << 20),
        cost_estimate=pl.CostEstimate(flops=2 * 256 * count * 2048 * 2048, bytes_accessed=10 << 20, transcendentals=0),
        name=name,
    )(factors, *pieces)


def products(ints, pieces, groups):
    x, c = lax.axis_index("x"), lax.axis_index("c")
    wide = ints[0].shape[2]
    ahead = jnp.where(c == 0, 3, 1)
    chunk = (x, (x + ahead) % 4, (x + 4 - ahead) % 4, (x + 2) % 4)
    where_int = [(i, n) for i in ints for n in range(i.shape[0])]
    for g in range(groups):
        total = None
        for (ref, inner), at in zip(where_int, chunk):
            at = pl.ds(pl.multiple_of(at * wide, wide), wide)
            side = jnp.concatenate([pieces[2 * g][:, at], pieces[2 * g + 1][:, at]], axis=0)
            value = lax.dot_general(ref[inner], side, (((1,), (1,)), ((), ())), preferred_element_type=jnp.float32)
            total = value if total is None else total + value
        yield total


def early_kernel(*refs):
    ints, pieces, out = refs[:3], refs[3:-1], refs[-1]
    for g, total in enumerate(products(ints, pieces, len(pieces) // 2)):
        for n in range(total.shape[1] // LANES):
            out[g, n] = total[:, n * LANES:(n + 1) * LANES]


def late_kernel(*refs):
    ints, pieces, before, out, spare = refs[:3], refs[3:-3], refs[-3], refs[-2], refs[-1]
    z, h, c = (lax.axis_index(a) for a in ("z", "yh", "c"))
    ahead = jnp.where(c == 0, 3, 1)
    here = (c, 1 - c)
    away = (1 - c, c)
    places = (
        (z, h, here), (z, 1 - h, here),
        ((z + ahead) % 4, h, here), ((z + 4 - ahead) % 4, h, away),
        ((z + ahead) % 4, 1 - h, here), ((z + 4 - ahead) % 4, 1 - h, away),
        ((z + 2) % 4, (h + c) % 2, here), ((z + 2) % 4, (h + 1 - c) % 2, away),
    )
    groups, parts, rows, _ = before.shape
    depth = parts * LANES
    for total in products(ints, pieces, 1):
        for n in range(parts):
            spare[n] = total[:, n * LANES:(n + 1) * LANES]
    small = rows // DB
    folds = depth // DB
    fold = (lax.broadcasted_iota(jnp.int32, (folds, depth), 1) // DB
            == lax.broadcasted_iota(jnp.int32, (folds, depth), 0)).astype(jnp.float32)
    lane = lax.broadcasted_iota(jnp.int32, (small, LANES), 1) % DB
    for g in range(groups + 1):
        columns = []
        for n in range(parts):
            source = before.at[g, n] if g < groups else spare.at[n]
            total = source[pl.ds(0, small, stride=DB), :]
            for d in range(1, DB):
                total = jnp.where(lane == d, source[pl.ds(d, small, stride=DB), :], total)
            columns.append(total)
        total = jnp.concatenate(columns, axis=1)
        total = jnp.where(c == 0, total, jnp.concatenate([total[small // 2:], total[:small // 2]], axis=0))
        total = lax.dot_general(fold, total, (((1,), (1,)), ((), ())),
                                precision=lax.Precision.HIGHEST, preferred_element_type=jnp.float32)
        total = total.reshape(4, folds // 4, small)
        for n in range(4):
            at_z, at_h, cores = places[2 * g + n // 2]
            out[at_z * 4 + at_h * 2 + cores[n % 2]] = total[n]


def contract(ints, pieces, before):
    rows, depth = ints[0].shape[1], 2 * pieces[0].shape[0]
    groups = len(pieces) // 2
    if before is None:
        out_shape = jax.ShapeDtypeStruct((groups, depth // LANES, rows, LANES), jnp.float32)
    else:
        out_shape = jax.ShapeDtypeStruct((16, 8, rows // DB), jnp.float32)
    given = list(ints) + list(pieces) + ([] if before is None else [before])
    return pl.pallas_call(
        early_kernel if before is None else late_kernel,
        out_shape=out_shape,
        in_specs=[IN_VMEM] * len(given),
        out_specs=IN_VMEM,
        scratch_shapes=[] if before is None else [pltpu.VMEM((depth // LANES, rows, LANES), jnp.float32)],
        compiler_params=pltpu.CompilerParams(vmem_limit_bytes=12 << 20),
        cost_estimate=pl.CostEstimate(
            flops=2 * rows * depth * 4096 * groups, bytes_accessed=8 << 20, transcendentals=0),
        name="contract_early" if before is None else "contract_late",
    )(*given)


def core_swap(x):
    return shift(x, "c", 1, 2)


def both_ways(x, axis):
    pairs = [(i * 2 + c, (i + (1 if c == 0 else 3)) % 4 * 2 + c) for i in range(4) for c in range(2)]
    return lax.ppermute(x, (axis, "c"), pairs)


def local(amplitudes, factors, pair_list, window_offsets, occupied_energy, virtual_energy):
    rows_here, cols_here, aux = factors.shape
    virt = amplitudes.shape[1]
    n_d = cols_here // DB
    c = lax.axis_index("c")
    held = pltpu.with_memory_space_constraint(factors, pltpu.VMEM)
    factors = pltpu.with_memory_space_constraint(factors, pltpu.HBM)

    def lay(first, second):
        both = jnp.stack([first, second]).reshape(2, 8, n_d, DB, 4, LANES)
        return both.transpose(0, 1, 3, 4, 2, 5).reshape(2 * 8 * DB, n_d * virt)

    tau = amplitudes[0].T.reshape(8, cols_here, virt)
    tau = lax.all_to_all(tau, PAIR, split_axis=0, concat_axis=0, tiled=True)
    mine, other = move_call(
        functools.partial(pick_kernel, rows_here), "pick", [(cols_here, aux)] * 2, 1, 2)(window_offsets, factors)
    swapped = core_swap(other)
    keep, send = move_call(
        functools.partial(halve_kernel, rows_here), "halve", [(cols_here // 2, aux)] * 2, 2, 2)(
            window_offsets, mine, swapped)
    send, tau = lax.optimization_barrier((send, tau))

    got = shift(send, "yh", 1, 2)
    got, tau = lax.optimization_barrier((got, tau))
    tau_h = shift(tau, "yh", 1, 2)
    tau = lay(tau, core_swap(tau))
    arow, = move_call(
        functools.partial(choose_kernel, rows_here), "choose", [(cols_here // 2, aux)], 2, 1)(window_offsets, keep, got)
    up, down, far = (shift(arow, "z", s, 4) for s in (1, -1, 2))
    arow, = move_call(
        functools.partial(choose_z_kernel, rows_here), "choose_z", [(cols_here // 2, aux)], 4, 1)(
            window_offsets, arow, up, down, far)
    arow, tau, tau_h = lax.optimization_barrier((arow, tau, tau_h))

    side_tau = both_ways(tau, "z")
    tau_h = lay(tau_h, core_swap(tau_h))
    up, down, far = (shift_y(arow, s) for s in (1, -1, 2))
    near, = move_call(place_kernel, "place", [(2 * cols_here, aux)], 4, 4, False)(arow, up, down, far)
    near, tau_h, side_tau = lax.optimization_barrier((near, tau_h, side_tau))

    side_h = both_ways(tau_h, "z")
    near_c = core_swap(near)
    side = both_ways(near, "x")
    ints_near, = integrals_of(held, [near, near_c], (0,), "integrals_near")
    near_c, ints_near = lax.optimization_barrier((near_c, ints_near))
    side_c = both_ways(near_c, "x")
    far, side_h = lax.optimization_barrier((side, side_h))
    far = both_ways(far, "x")
    far_tau = both_ways(jnp.where(c == 0, side_tau, side_h), "z")
    pieces = [tau, tau_h, side_tau, core_swap(side_tau), side_h, core_swap(side_h)]
    ints_side, = integrals_of(
        held, [side, side_c, core_swap(side), core_swap(side_c)], (0, 1), "integrals_side")
    far, far_c, ints_side = lax.optimization_barrier((far, core_swap(far), ints_side))
    ints_far, = integrals_of(held, [far, far_c], (0,), "integrals_far")
    ints = [ints_near, ints_side, ints_far]
    partial = contract(ints, pieces, None)
    far_tau, partial = lax.optimization_barrier((far_tau, partial))
    partial = contract(ints, [far_tau, core_swap(far_tau)], partial)

    parts = lax.all_to_all(partial.reshape(128, 2 * rows_here), TILE + PAIR, split_axis=0, concat_axis=0, tiled=True)
    residual = parts.reshape(16, 8, 2, rows_here).sum(axis=1).transpose(1, 0, 2).reshape(1, 2, 16 * rows_here)
    occupied_sum = lookup(occupied_energy, pair_list[:, 0]) + lookup(occupied_energy, pair_list[:, 1])
    window_energy = lookup(virtual_energy, window_offsets)
    denominator = (
        window_energy[None, :, None] + virtual_energy[None, None, :] - occupied_sum[:, None, None]
    )
    return residual, residual / denominator


def solution(mesh):
    fine = Mesh(mesh.devices.reshape(4, 2, 4, 2, 2), PAIR + TILE)
    return jax.shard_map(
        local,
        mesh=fine,
        in_specs=(P(PAIR + TILE, None, None), P(TILE, PAIR, None), P(PAIR + TILE, None), P(), P(), P()),
        out_specs=(P(PAIR + TILE, None, None), P(PAIR + TILE, None, None)),
        check_vma=False,
    )
```

```python
import functools

import jax
import jax.numpy as jnp
from jax import lax
from jax.experimental import pallas as pl
from jax.experimental.pallas import tpu as pltpu
from jax.sharding import Mesh, PartitionSpec as P

PAIR = ("x", "yl")
TILE = ("z", "yh", "c")
DB = 8
LANES = 128


def shift(x, axis, step, size):
    return lax.ppermute(x, axis, [(i, (i + step) % size) for i in range(size)])


def shift_y(x, step):
    at = [y % 2 * 2 + y // 2 for y in range(4)]
    return lax.ppermute(x, ("yl", "yh"), [(at[y], at[(y + step) % 4]) for y in range(4)])


def pick_kernel(rows, offsets, factors, mine, other, sem):
    c = lax.axis_index("c")
    first = pltpu.make_async_copy(factors.at[offsets[c] % rows], mine, sem.at[0])
    second = pltpu.make_async_copy(factors.at[offsets[1 - c] % rows], other, sem.at[1])
    first.start()
    second.start()
    first.wait()
    second.wait()


def halve_kernel(rows, offsets, mine, swapped, keep, send, sem):
    c, h = lax.axis_index("c"), lax.axis_index("yh")
    size = keep.shape[0]

    def move(source):
        first = pltpu.make_async_copy(source.at[pl.ds(h * size, size), :], keep, sem.at[0])
        second = pltpu.make_async_copy(source.at[pl.ds((1 - h) * size, size), :], send, sem.at[1])
        first.start()
        second.start()
        first.wait()
        second.wait()

    here = offsets[c] // rows % 2 == c

    @pl.when(here)
    def _():
        move(mine)

    @pl.when(jnp.logical_not(here))
    def _():
        move(swapped)


def choose_kernel(rows, offsets, keep, got, out, sem):
    here = offsets[lax.axis_index("c")] // (2 * rows) % 2 == lax.axis_index("yh")
    for source, wanted in ((keep, here), (got, jnp.logical_not(here))):
        @pl.when(wanted)
        def _():
            copy = pltpu.make_async_copy(source, out, sem.at[0])
            copy.start()
            copy.wait()


def choose_z_kernel(rows, offsets, own, up, down, far, out, sem):
    rel = (offsets[lax.axis_index("c")] // (4 * rows) + 4 - lax.axis_index("z")) % 4
    for source, wanted in ((own, 0), (down, 1), (far, 2), (up, 3)):
        @pl.when(rel == wanted)
        def _():
            copy = pltpu.make_async_copy(source, out, sem.at[0])
            copy.start()
            copy.wait()


def lay_kernel(first, second, out):
    count, depth, width = first.shape
    wide = depth // DB * LANES
    for half, piece in enumerate((first, second)):
        for i in range(count):
            row = (half * count + i) * DB
            for d in range(depth // DB):
                block = piece[i, d * DB:(d + 1) * DB, :]
                for n in range(width // LANES):
                    at = n * wide + d * LANES
                    out[row:row + DB, at:at + LANES] = block[:, n * LANES:(n + 1) * LANES]


def lay(first, second):
    count, depth, width = first.shape
    return pl.pallas_call(
        lay_kernel,
        out_shape=jax.ShapeDtypeStruct((2 * count * DB, depth // DB * width), jnp.bfloat16),
        in_specs=[IN_VMEM] * 2,
        out_specs=IN_VMEM,
        compiler_params=pltpu.CompilerParams(vmem_limit_bytes=4 << 20),
        cost_estimate=pl.CostEstimate(flops=0, bytes_accessed=2 << 20, transcendentals=0),
        name="lay",
    )(first, second)


def take_kernel(source, out, sem):
    copy = pltpu.make_async_copy(source.at[pl.ds(0, out.shape[0]), :], out, sem.at[0])
    copy.start()
    copy.wait()


def place_kernel(own, up, down, far, out, sem):
    y = lax.axis_index("yh") * 2 + lax.axis_index("yl")
    size = own.shape[0]
    copies = []
    for n, (piece, step) in enumerate(((own, 0), (up, 3), (down, 1), (far, 2))):
        at = (y + step) % 4
        at = at % 2 * 2 + at // 2
        copies.append(pltpu.make_async_copy(piece, out.at[pl.ds(at * size, size), :], sem.at[n]))
    for copy in copies:
        copy.start()
    for copy in copies:
        copy.wait()


ANY = pl.BlockSpec(memory_space=pl.ANY)
SMALL = pl.BlockSpec(memory_space=pltpu.SMEM)


def move_call(body, name, shapes, n_in, n_sem, small=True):
    specs = ([SMALL] if small else []) + [ANY] * n_in
    return pl.pallas_call(
        body,
        out_shape=[jax.ShapeDtypeStruct(shape, jnp.bfloat16) for shape in shapes],
        in_specs=specs,
        out_specs=[ANY] * len(shapes),
        scratch_shapes=[pltpu.SemaphoreType.DMA((n_sem,))],
        compiler_params=pltpu.CompilerParams(vmem_limit_bytes=1 << 20),
        cost_estimate=pl.CostEstimate(flops=0, bytes_accessed=1 << 20, transcendentals=0),
        name=name,
    )


def integrals(held, pieces, flips, out):
    rows, cols, aux = held.shape
    deep = 2 * DB
    side = [p[...] for p in pieces]
    side = jnp.concatenate(side, axis=0)
    for step in range(cols // deep):
        yield step
        slab = held[:, step * deep:(step + 1) * deep, :].reshape(rows * deep, aux)
        value = lax.dot_general(slab, side, (((1,), (1,)), ((), ())), preferred_element_type=jnp.float32)
        value = value.astype(jnp.bfloat16).reshape(rows, deep // DB, DB, side.shape[0])
        for n in range(side.shape[0] // LANES):
            k = (n + flips[n // 2]) % 2
            for d in range(deep // DB):
                block = value[:, d, :, n * LANES:(n + 1) * LANES].reshape(rows * DB, LANES)
                at = step * deep // DB + d
                out[n // 2, k * rows * DB:(k + 1) * rows * DB, at * LANES:(at + 1) * LANES] = block


def first_kernel(factors, first, second, out, held, sem):
    deep = 2 * DB
    copies = []
    for step in range(held.shape[1] // deep):
        part = pl.ds(step * deep, deep)
        copies.append(pltpu.make_async_copy(factors.at[:, part, :], held.at[:, part, :], sem.at[step]))
        copies[-1].start()
    for step in integrals(held, (first, second), (0,), out):
        copies[step].wait()


def next_kernel(flips, held, *refs):
    for _ in integrals(held, refs[:-1], flips, refs[-1]):
        pass


IN_VMEM = pl.BlockSpec(memory_space=pltpu.VMEM)
IN_HBM = pl.BlockSpec(memory_space=pltpu.HBM)


def integrals_of(factors, pieces, flips, name, load=False):
    rows, cols, aux = factors.shape
    count = len(flips)
    out_shape = [jax.ShapeDtypeStruct((count, 2 * rows * DB, cols // DB * LANES), jnp.bfloat16)]
    if load:
        out_shape.append(jax.ShapeDtypeStruct(factors.shape, factors.dtype))
    return pl.pallas_call(
        first_kernel if load else functools.partial(next_kernel, flips),
        out_shape=out_shape,
        in_specs=[IN_HBM if load else IN_VMEM] + [IN_VMEM] * len(pieces),
        out_specs=[IN_VMEM] * len(out_shape),
        scratch_shapes=[pltpu.SemaphoreType.DMA((4,))] if load else [],
        compiler_params=pltpu.CompilerParams(vmem_limit_bytes=12 << 20),
        cost_estimate=pl.CostEstimate(flops=2 * 256 * count * 2048 * 2048, bytes_accessed=10 << 20, transcendentals=0),
        name=name,
    )(factors, *pieces)


def products(ints, pieces, groups):
    x, c = lax.axis_index("x"), lax.axis_index("c")
    wide = ints[0].shape[2]
    ahead = jnp.where(c == 0, 3, 1)
    chunk = (x, (x + ahead) % 4, (x + 4 - ahead) % 4, (x + 2) % 4)
    where_int = [(i, n) for i in ints for n in range(i.shape[0])]
    each = len(pieces) // groups
    for g in range(groups):
        total = None
        for (ref, inner), at in zip(where_int, chunk):
            at = pl.ds(pl.multiple_of(at * wide, wide), wide)
            side = jnp.concatenate([p[:, at] for p in pieces[each * g:each * (g + 1)]], axis=0)
            value = lax.dot_general(ref[inner], side, (((1,), (1,)), ((), ())), preferred_element_type=jnp.float32)
            total = value if total is None else total + value
        yield total


def early_kernel(*refs):
    ints, pieces, out = refs[:3], refs[3:-1], refs[-1]
    for g, total in enumerate(products(ints, pieces, out.shape[0])):
        for n in range(total.shape[1] // LANES):
            out[g, n] = total[:, n * LANES:(n + 1) * LANES]


def late_kernel(*refs):
    ints, pieces, before, out, spare = refs[:3], refs[3:-3], refs[-3], refs[-2], refs[-1]
    z, h, c = (lax.axis_index(a) for a in ("z", "yh", "c"))
    ahead = jnp.where(c == 0, 3, 1)
    here = (c, 1 - c)
    away = (1 - c, c)
    places = (
        (z, h, here), (z, 1 - h, here),
        ((z + ahead) % 4, h, here), ((z + 4 - ahead) % 4, h, away),
        ((z + ahead) % 4, 1 - h, here), ((z + 4 - ahead) % 4, 1 - h, away),
        ((z + 2) % 4, h, here), ((z + 2) % 4, 1 - h, here),
    )
    groups, parts, rows, _ = before.shape
    depth = parts * LANES
    for total in products(ints, pieces, 1):
        for n in range(parts):
            spare[n] = total[:, n * LANES:(n + 1) * LANES]
    small = rows // DB
    folds = depth // DB
    fold = (lax.broadcasted_iota(jnp.int32, (folds, depth), 1) // DB
            == lax.broadcasted_iota(jnp.int32, (folds, depth), 0)).astype(jnp.float32)
    lane = lax.broadcasted_iota(jnp.int32, (small, LANES), 1) % DB
    for g in range(groups + 1):
        columns = []
        for n in range(parts):
            source = before.at[g, n] if g < groups else spare.at[n]
            total = source[pl.ds(0, small, stride=DB), :]
            for d in range(1, DB):
                total = jnp.where(lane == d, source[pl.ds(d, small, stride=DB), :], total)
            columns.append(total)
        total = jnp.concatenate(columns, axis=1)
        total = jnp.where(c == 0, total, jnp.concatenate([total[small // 2:], total[:small // 2]], axis=0))
        total = lax.dot_general(fold, total, (((1,), (1,)), ((), ())),
                                precision=lax.Precision.HIGHEST, preferred_element_type=jnp.float32)
        total = total.reshape(4, folds // 4, small)
        for n in range(4):
            at_z, at_h, cores = places[2 * g + n // 2]
            out[at_z * 4 + at_h * 2 + cores[n % 2]] = total[n]


def contract(ints, pieces, before):
    rows, depth = ints[0].shape[1], 256
    groups = sum(p.shape[0] for p in pieces) // depth
    if before is None:
        out_shape = jax.ShapeDtypeStruct((groups, depth // LANES, rows, LANES), jnp.float32)
    else:
        out_shape = jax.ShapeDtypeStruct((16, 8, rows // DB), jnp.float32)
    given = list(ints) + list(pieces) + ([] if before is None else [before])
    return pl.pallas_call(
        early_kernel if before is None else late_kernel,
        out_shape=out_shape,
        in_specs=[IN_VMEM] * len(given),
        out_specs=IN_VMEM,
        scratch_shapes=[] if before is None else [pltpu.VMEM((depth // LANES, rows, LANES), jnp.float32)],
        compiler_params=pltpu.CompilerParams(vmem_limit_bytes=12 << 20),
        cost_estimate=pl.CostEstimate(
            flops=2 * rows * depth * 4096 * groups, bytes_accessed=8 << 20, transcendentals=0),
        name="contract_early" if before is None else "contract_late",
    )(*given)


def finish_kernel(pairs, offsets, occupied, virtual, parts, energies, residual, update):
    count, width = parts.shape
    total = parts[...].reshape(16, count // 16, width).sum(axis=1)
    wide = width // 2
    occupied_sum = occupied[pairs[0, 0]] + occupied[pairs[0, 1]]
    every = energies[...].reshape(1, energies.shape[0])
    for k in range(2):
        row = jnp.concatenate([total[n:n + 1, k * wide:(k + 1) * wide] for n in range(16)], axis=1)
        residual[0, k:k + 1, :] = row
        update[0, k:k + 1, :] = row / (virtual[offsets[k]] + every - occupied_sum)


def core_swap(x):
    return shift(x, "c", 1, 2)


def both_ways(x, axis):
    pairs = [(i * 2 + c, (i + (1 if c == 0 else 3)) % 4 * 2 + c) for i in range(4) for c in range(2)]
    return lax.ppermute(x, (axis, "c"), pairs)


def local(amplitudes, factors, pair_list, window_offsets, occupied_energy, virtual_energy):
    rows_here, cols_here, aux = factors.shape
    virt = amplitudes.shape[1]
    n_d = cols_here // DB
    c = lax.axis_index("c")
    held = pltpu.with_memory_space_constraint(factors, pltpu.VMEM)
    factors = pltpu.with_memory_space_constraint(factors, pltpu.HBM)

    tau = amplitudes[0].T.reshape(8, cols_here, virt)
    tau = lax.all_to_all(tau, PAIR, split_axis=0, concat_axis=0, tiled=True)
    mine, other = move_call(
        functools.partial(pick_kernel, rows_here), "pick", [(cols_here, aux)] * 2, 1, 2)(window_offsets, factors)
    swapped = core_swap(other)
    keep, send = move_call(
        functools.partial(halve_kernel, rows_here), "halve", [(cols_here // 2, aux)] * 2, 2, 2)(
            window_offsets, mine, swapped)

    got = shift(send, "yh", 1, 2)
    arow, = move_call(
        functools.partial(choose_kernel, rows_here), "choose", [(cols_here // 2, aux)], 2, 1)(window_offsets, keep, got)
    arow, tau = lax.optimization_barrier((arow, tau))
    tau_h = shift(tau, "yh", 1, 2)
    tau = lay(tau, core_swap(tau))
    up, down, far = (shift(arow, "z", s, 4) for s in (1, -1, 2))
    arow, = move_call(
        functools.partial(choose_z_kernel, rows_here), "choose_z", [(cols_here // 2, aux)], 4, 1)(
            window_offsets, arow, up, down, far)
    arow, tau, tau_h = lax.optimization_barrier((arow, tau, tau_h))

    side_tau = both_ways(tau, "z")
    tau_h = lay(tau_h, core_swap(tau_h))
    up, down, far = (shift_y(arow, s) for s in (1, -1, 2))
    near, = move_call(place_kernel, "place", [(2 * cols_here, aux)], 4, 4, False)(arow, up, down, far)
    near, tau_h, side_tau = lax.optimization_barrier((near, tau_h, side_tau))

    side_h = both_ways(tau_h, "z")
    near_c = core_swap(near)
    side = both_ways(near, "x")
    take = move_call(take_kernel, "take", [(tau.shape[0] // 2, tau.shape[1])], 1, 1, False)
    far_tau = both_ways(take(side_tau)[0], "z")
    ints_near, = integrals_of(held, [near, near_c], (0,), "integrals_near")
    near_c, ints_near = lax.optimization_barrier((near_c, ints_near))
    side_c = both_ways(near_c, "x")
    far = both_ways(side, "x")
    held, side_h, far_tau = lax.optimization_barrier((held, side_h, far_tau))
    far_h = both_ways(take(side_h)[0], "z")
    ints_side, = integrals_of(
        held, [side, side_c, core_swap(side), core_swap(side_c)], (0, 1), "integrals_side")
    far, far_c, ints_side = lax.optimization_barrier((far, core_swap(far), ints_side))
    ints_far, = integrals_of(held, [far, far_c], (0,), "integrals_far")
    ints = [ints_near, ints_side, ints_far]
    pieces = [tau, tau_h, side_tau, core_swap(side_tau), side_h, core_swap(side_h)]
    partial = contract(ints, pieces, None)

    far_h, partial = lax.optimization_barrier((far_h, partial))
    partial = contract(ints, [far_tau, core_swap(far_tau), far_h, core_swap(far_h)], partial)

    parts = lax.all_to_all(partial.reshape(128, 2 * rows_here), TILE + PAIR, split_axis=0, concat_axis=0, tiled=True)
    residual, update = pl.pallas_call(
        finish_kernel,
        out_shape=[jax.ShapeDtypeStruct((1, 2, 16 * rows_here), jnp.float32)] * 2,
        in_specs=[SMALL] * 4 + [IN_VMEM] * 2,
        out_specs=[IN_VMEM] * 2,
        compiler_params=pltpu.CompilerParams(vmem_limit_bytes=1 << 20),
        name="finish",
    )(pair_list, window_offsets, occupied_energy, virtual_energy, parts, virtual_energy)
    return residual, update


def solution(mesh):
    fine = Mesh(mesh.devices.reshape(4, 2, 4, 2, 2), PAIR + TILE)
    return jax.shard_map(
        local,
        mesh=fine,
        in_specs=(P(PAIR + TILE, None, None), P(TILE, PAIR, None), P(PAIR + TILE, None), P(), P(), P()),
        out_specs=(P(PAIR + TILE, None, None), P(PAIR + TILE, None, None)),
        check_vma=False,
    )
```

```python
import functools

import jax
import jax.numpy as jnp
from jax import lax
from jax.experimental import pallas as pl
from jax.experimental.pallas import tpu as pltpu
from jax.sharding import Mesh, PartitionSpec as P

PAIR = ("x", "yl")
TILE = ("z", "yh", "c")
DB = 8
LANES = 128


def shift(x, axis, step, size):
    return lax.ppermute(x, axis, [(i, (i + step) % size) for i in range(size)])


def shift_y(x, step):
    at = [y % 2 * 2 + y // 2 for y in range(4)]
    return lax.ppermute(x, ("yl", "yh"), [(at[y], at[(y + step) % 4]) for y in range(4)])


def pick_kernel(rows, offsets, factors, mine, other, sem):
    c = lax.axis_index("c")
    first = pltpu.make_async_copy(factors.at[offsets[c] % rows], mine, sem.at[0])
    second = pltpu.make_async_copy(factors.at[offsets[1 - c] % rows], other, sem.at[1])
    first.start()
    second.start()
    first.wait()
    second.wait()


def halve_kernel(rows, offsets, mine, swapped, keep, send, sem):
    c, h = lax.axis_index("c"), lax.axis_index("yh")
    size = keep.shape[0]

    def move(source):
        first = pltpu.make_async_copy(source.at[pl.ds(h * size, size), :], keep, sem.at[0])
        second = pltpu.make_async_copy(source.at[pl.ds((1 - h) * size, size), :], send, sem.at[1])
        first.start()
        second.start()
        first.wait()
        second.wait()

    here = offsets[c] // rows % 2 == c

    @pl.when(here)
    def _():
        move(mine)

    @pl.when(jnp.logical_not(here))
    def _():
        move(swapped)


def choose_kernel(rows, offsets, keep, got, out, sem):
    here = offsets[lax.axis_index("c")] // (2 * rows) % 2 == lax.axis_index("yh")
    for source, wanted in ((keep, here), (got, jnp.logical_not(here))):
        @pl.when(wanted)
        def _():
            copy = pltpu.make_async_copy(source, out, sem.at[0])
            copy.start()
            copy.wait()


def choose_z_kernel(rows, offsets, own, up, down, far, out, sem):
    rel = (offsets[lax.axis_index("c")] // (4 * rows) + 4 - lax.axis_index("z")) % 4
    for source, wanted in ((own, 0), (down, 1), (far, 2), (up, 3)):
        @pl.when(rel == wanted)
        def _():
            copy = pltpu.make_async_copy(source, out, sem.at[0])
            copy.start()
            copy.wait()


def lay_kernel(first, second, out):
    count, depth, width = first.shape
    wide = depth // DB * LANES
    for half, piece in enumerate((first, second)):
        for i in range(count):
            row = (half * count + i) * DB
            for d in range(depth // DB):
                block = piece[i, d * DB:(d + 1) * DB, :]
                for n in range(width // LANES):
                    at = n * wide + d * LANES
                    out[row:row + DB, at:at + LANES] = block[:, n * LANES:(n + 1) * LANES]


def lay(first, second):
    count, depth, width = first.shape
    return pl.pallas_call(
        lay_kernel,
        out_shape=jax.ShapeDtypeStruct((2 * count * DB, depth // DB * width), jnp.bfloat16),
        in_specs=[IN_VMEM] * 2,
        out_specs=IN_VMEM,
        compiler_params=pltpu.CompilerParams(vmem_limit_bytes=4 << 20),
        cost_estimate=pl.CostEstimate(flops=0, bytes_accessed=2 << 20, transcendentals=0),
        name="lay",
    )(first, second)


def take_kernel(source, out, sem):
    copy = pltpu.make_async_copy(source.at[pl.ds(0, out.shape[0]), :], out, sem.at[0])
    copy.start()
    copy.wait()


def hold_kernel(source, out, sem):
    copy = pltpu.make_async_copy(source, out, sem.at[0])
    copy.start()
    copy.wait()


def hold(factors):
    return pl.pallas_call(
        hold_kernel,
        out_shape=jax.ShapeDtypeStruct(factors.shape, factors.dtype),
        in_specs=[IN_HBM],
        out_specs=IN_VMEM,
        scratch_shapes=[pltpu.SemaphoreType.DMA((1,))],
        compiler_params=pltpu.CompilerParams(vmem_limit_bytes=1 << 20),
        cost_estimate=pl.CostEstimate(flops=0, bytes_accessed=16 << 20, transcendentals=0),
        name="hold",
    )(factors)


def place_kernel(own, up, down, far, out, sem):
    y = lax.axis_index("yh") * 2 + lax.axis_index("yl")
    size = own.shape[0]
    copies = []
    for n, (piece, step) in enumerate(((own, 0), (up, 3), (down, 1), (far, 2))):
        at = (y + step) % 4
        at = at % 2 * 2 + at // 2
        copies.append(pltpu.make_async_copy(piece, out.at[pl.ds(at * size, size), :], sem.at[n]))
    for copy in copies:
        copy.start()
    for copy in copies:
        copy.wait()


ANY = pl.BlockSpec(memory_space=pl.ANY)
SMALL = pl.BlockSpec(memory_space=pltpu.SMEM)


def move_call(body, name, shapes, n_in, n_sem, small=True):
    specs = ([SMALL] if small else []) + [ANY] * n_in
    return pl.pallas_call(
        body,
        out_shape=[jax.ShapeDtypeStruct(shape, jnp.bfloat16) for shape in shapes],
        in_specs=specs,
        out_specs=[ANY] * len(shapes),
        scratch_shapes=[pltpu.SemaphoreType.DMA((n_sem,))],
        compiler_params=pltpu.CompilerParams(vmem_limit_bytes=1 << 20),
        cost_estimate=pl.CostEstimate(flops=0, bytes_accessed=1 << 20, transcendentals=0),
        name=name,
    )


def integrals(held, pieces, flips, out):
    rows, cols, aux = held.shape
    deep = 2 * DB
    side = [p[...] for p in pieces]
    side = jnp.concatenate(side, axis=0)
    for step in range(cols // deep):
        yield step
        slab = held[:, step * deep:(step + 1) * deep, :].reshape(rows * deep, aux)
        value = lax.dot_general(slab, side, (((1,), (1,)), ((), ())), preferred_element_type=jnp.float32)
        value = value.astype(jnp.bfloat16).reshape(rows, deep // DB, DB, side.shape[0])
        for n in range(side.shape[0] // LANES):
            k = (n + flips[n // 2]) % 2
            for d in range(deep // DB):
                block = value[:, d, :, n * LANES:(n + 1) * LANES].reshape(rows * DB, LANES)
                at = step * deep // DB + d
                out[n // 2, k * rows * DB:(k + 1) * rows * DB, at * LANES:(at + 1) * LANES] = block


def first_kernel(factors, first, second, out, held, sem):
    deep = 2 * DB
    copies = []
    for step in range(held.shape[1] // deep):
        part = pl.ds(step * deep, deep)
        copies.append(pltpu.make_async_copy(factors.at[:, part, :], held.at[:, part, :], sem.at[step]))
        copies[-1].start()
    for step in integrals(held, (first, second), (0,), out):
        copies[step].wait()


def next_kernel(flips, held, *refs):
    for _ in integrals(held, refs[:-1], flips, refs[-1]):
        pass


IN_VMEM = pl.BlockSpec(memory_space=pltpu.VMEM)
IN_HBM = pl.BlockSpec(memory_space=pltpu.HBM)


def integrals_of(factors, pieces, flips, name, load=False):
    rows, cols, aux = factors.shape
    count = len(flips)
    out_shape = [jax.ShapeDtypeStruct((count, 2 * rows * DB, cols // DB * LANES), jnp.bfloat16)]
    if load:
        out_shape.append(jax.ShapeDtypeStruct(factors.shape, factors.dtype))
    return pl.pallas_call(
        first_kernel if load else functools.partial(next_kernel, flips),
        out_shape=out_shape,
        in_specs=[IN_HBM if load else IN_VMEM] + [IN_VMEM] * len(pieces),
        out_specs=[IN_VMEM] * len(out_shape),
        scratch_shapes=[pltpu.SemaphoreType.DMA((4,))] if load else [],
        compiler_params=pltpu.CompilerParams(vmem_limit_bytes=12 << 20),
        cost_estimate=pl.CostEstimate(flops=2 * 256 * count * 2048 * 2048, bytes_accessed=10 << 20, transcendentals=0),
        name=name,
    )(factors, *pieces)


def products(ints, chunks, pieces):
    x, c = lax.axis_index("x"), lax.axis_index("c")
    wide = ints[0].shape[2]
    ahead = jnp.where(c == 0, 3, 1)
    chunk = (x, (x + ahead) % 4, (x + 4 - ahead) % 4, (x + 2) % 4)
    where_int = [(i, n) for i in ints for n in range(i.shape[0])]
    total = None
    for (ref, inner), at in zip(where_int, chunks):
        at = pl.ds(pl.multiple_of(chunk[at] * wide, wide), wide)
        side = jnp.concatenate([p[:, at] for p in pieces], axis=0)
        value = lax.dot_general(ref[inner], side, (((1,), (1,)), ((), ())), preferred_element_type=jnp.float32)
        total = value if total is None else total + value
    return total


def early_kernel(*refs):
    ints, pieces, out = refs[:2], refs[2:-1], refs[-1]
    for g in range(out.shape[0]):
        total = products(ints, (0, 1, 2), pieces[2 * g:2 * g + 2])
        for n in range(total.shape[1] // LANES):
            out[g, n] = total[:, n * LANES:(n + 1) * LANES]


def late_kernel(*refs):
    ints, pieces, before, out, spare = refs[:3], refs[3:-3], refs[-3], refs[-2], refs[-1]
    z, h, c = (lax.axis_index(a) for a in ("z", "yh", "c"))
    ahead = jnp.where(c == 0, 3, 1)
    here = (c, 1 - c)
    away = (1 - c, c)
    places = (
        (z, h, here), (z, 1 - h, here),
        ((z + ahead) % 4, h, here), ((z + 4 - ahead) % 4, h, away),
        ((z + ahead) % 4, 1 - h, here), ((z + 4 - ahead) % 4, 1 - h, away),
        ((z + 2) % 4, h, here), ((z + 2) % 4, 1 - h, here),
    )
    groups, parts, rows, _ = before.shape
    depth = parts * LANES
    for g in range(groups + 1):
        if g < groups:
            total = products(ints[2:], (3,), pieces[2 * g:2 * g + 2])
        else:
            total = products(ints, (0, 1, 2, 3), pieces[2 * groups:])
        for n in range(parts):
            value = total[:, n * LANES:(n + 1) * LANES]
            spare[g, n] = value + before[g, n] if g < groups else value
    small = rows // DB
    folds = depth // DB
    fold = (lax.broadcasted_iota(jnp.int32, (folds, depth), 1) // DB
            == lax.broadcasted_iota(jnp.int32, (folds, depth), 0)).astype(jnp.float32)
    lane = lax.broadcasted_iota(jnp.int32, (small, LANES), 1) % DB
    for g in range(groups + 1):
        columns = []
        for n in range(parts):
            source = spare.at[g, n]
            total = source[pl.ds(0, small, stride=DB), :]
            for d in range(1, DB):
                total = jnp.where(lane == d, source[pl.ds(d, small, stride=DB), :], total)
            columns.append(total)
        total = jnp.concatenate(columns, axis=1)
        total = jnp.where(c == 0, total, jnp.concatenate([total[small // 2:], total[:small // 2]], axis=0))
        total = lax.dot_general(fold, total, (((1,), (1,)), ((), ())),
                                precision=lax.Precision.HIGHEST, preferred_element_type=jnp.float32)
        total = total.reshape(4, folds // 4, small)
        for n in range(4):
            at_z, at_h, cores = places[2 * g + n // 2]
            out[at_z * 4 + at_h * 2 + cores[n % 2]] = total[n]


def contract(ints, pieces, before):
    rows, depth = ints[0].shape[1], 256
    groups = sum(p.shape[0] for p in pieces) // depth
    kept = jax.ShapeDtypeStruct((groups, depth // LANES, rows, LANES), jnp.float32)
    if before is None:
        out_shape = kept
    else:
        out_shape = jax.ShapeDtypeStruct((16, 8, rows // DB), jnp.float32)
    given = list(ints) + list(pieces) + ([] if before is None else [before])
    return pl.pallas_call(
        early_kernel if before is None else late_kernel,
        out_shape=out_shape,
        in_specs=[IN_VMEM] * len(given),
        out_specs=IN_VMEM,
        scratch_shapes=[] if before is None else [pltpu.VMEM(kept.shape, kept.dtype)],
        compiler_params=pltpu.CompilerParams(vmem_limit_bytes=12 << 20),
        cost_estimate=pl.CostEstimate(
            flops=2 * rows * depth * 1024 * (9 if before is None else 7), bytes_accessed=8 << 20, transcendentals=0),
        name="contract_early" if before is None else "contract_late",
    )(*given)


def finish_kernel(pairs, offsets, occupied, virtual, parts, energies, residual, update):
    count, width = parts.shape
    total = parts[...].reshape(16, count // 16, width).sum(axis=1)
    wide = width // 2
    occupied_sum = occupied[pairs[0, 0]] + occupied[pairs[0, 1]]
    every = energies[...].reshape(1, energies.shape[0])
    for k in range(2):
        row = jnp.concatenate([total[n:n + 1, k * wide:(k + 1) * wide] for n in range(16)], axis=1)
        residual[0, k:k + 1, :] = row
        update[0, k:k + 1, :] = row / (virtual[offsets[k]] + every - occupied_sum)


def core_swap(x):
    return shift(x, "c", 1, 2)


def both_ways(x, axis):
    pairs = [(i * 2 + c, (i + (1 if c == 0 else 3)) % 4 * 2 + c) for i in range(4) for c in range(2)]
    return lax.ppermute(x, (axis, "c"), pairs)


def local(amplitudes, factors, pair_list, window_offsets, occupied_energy, virtual_energy):
    rows_here, cols_here, aux = factors.shape
    virt = amplitudes.shape[1]
    n_d = cols_here // DB
    c = lax.axis_index("c")
    factors = pltpu.with_memory_space_constraint(factors, pltpu.HBM)

    tau = amplitudes[0].T.reshape(8, cols_here, virt)
    tau = lax.all_to_all(tau, PAIR, split_axis=0, concat_axis=0, tiled=True)
    mine, other = move_call(
        functools.partial(pick_kernel, rows_here), "pick", [(cols_here, aux)] * 2, 1, 2)(window_offsets, factors)
    swapped = core_swap(other)
    keep, send = move_call(
        functools.partial(halve_kernel, rows_here), "halve", [(cols_here // 2, aux)] * 2, 2, 2)(
            window_offsets, mine, swapped)

    got = shift(send, "yh", 1, 2)
    arow, = move_call(
        functools.partial(choose_kernel, rows_here), "choose", [(cols_here // 2, aux)], 2, 1)(window_offsets, keep, got)
    arow, tau = lax.optimization_barrier((arow, tau))
    tau_h = shift(tau, "yh", 1, 2)
    tau = lay(tau, core_swap(tau))
    arow, factors = lax.optimization_barrier((arow, factors))
    held = hold(factors)
    up, down, far = (shift(arow, "z", s, 4) for s in (1, -1, 2))
    arow, = move_call(
        functools.partial(choose_z_kernel, rows_here), "choose_z", [(cols_here // 2, aux)], 4, 1)(
            window_offsets, arow, up, down, far)
    arow, tau, tau_h, held = lax.optimization_barrier((arow, tau, tau_h, held))

    side_tau = both_ways(tau, "z")
    tau_h = lay(tau_h, core_swap(tau_h))
    side_h = both_ways(tau_h, "z")
    up, down, far = (shift_y(arow, s) for s in (1, -1, 2))
    near, = move_call(place_kernel, "place", [(2 * cols_here, aux)], 4, 4, False)(arow, up, down, far)
    near, tau_h = lax.optimization_barrier((near, tau_h))

    near_c = core_swap(near)
    side = both_ways(near, "x")
    side_c = both_ways(near_c, "x")
    held, side_tau, side_h = lax.optimization_barrier((held, side_tau, side_h))
    take = move_call(take_kernel, "take", [(tau.shape[0] // 2, tau.shape[1])], 1, 1, False)
    far_tau = both_ways(take(side_tau)[0], "z")
    far_h = both_ways(take(side_h)[0], "z")
    ints_near, = integrals_of(held, [near, near_c], (0,), "integrals_near")
    side, side_c, ints_near = lax.optimization_barrier((side, side_c, ints_near))
    far = both_ways(side, "x")
    ints_side, = integrals_of(
        held, [side, side_c, core_swap(side), core_swap(side_c)], (0, 1), "integrals_side")
    pieces = [tau, tau_h, side_tau, core_swap(side_tau), side_h, core_swap(side_h)]
    partial = contract([ints_near, ints_side], pieces, None)
    far, partial = lax.optimization_barrier((far, partial))
    ints_far, = integrals_of(held, [far, core_swap(far)], (0,), "integrals_far")
    pieces += [far_tau, core_swap(far_tau), far_h, core_swap(far_h)]
    partial = contract([ints_near, ints_side, ints_far], pieces, partial)

    parts = lax.all_to_all(partial.reshape(128, 2 * rows_here), TILE + PAIR, split_axis=0, concat_axis=0, tiled=True)
    residual, update = pl.pallas_call(
        finish_kernel,
        out_shape=[jax.ShapeDtypeStruct((1, 2, 16 * rows_here), jnp.float32)] * 2,
        in_specs=[SMALL] * 4 + [IN_VMEM] * 2,
        out_specs=[IN_VMEM] * 2,
        compiler_params=pltpu.CompilerParams(vmem_limit_bytes=1 << 20),
        name="finish",
    )(pair_list, window_offsets, occupied_energy, virtual_energy, parts, virtual_energy)
    return residual, update


def solution(mesh):
    fine = Mesh(mesh.devices.reshape(4, 2, 4, 2, 2), PAIR + TILE)
    return jax.shard_map(
        local,
        mesh=fine,
        in_specs=(P(PAIR + TILE, None, None), P(TILE, PAIR, None), P(PAIR + TILE, None), P(), P(), P()),
        out_specs=(P(PAIR + TILE, None, None), P(PAIR + TILE, None, None)),
        check_vma=False,
    )
```

```python
import functools

import jax
import jax.numpy as jnp
from jax import lax
from jax.experimental import pallas as pl
from jax.experimental.pallas import tpu as pltpu
from jax.sharding import Mesh, PartitionSpec as P

PAIR = ("x", "yl")
TILE = ("z", "yh", "c")
DB = 8
LANES = 128


def shift(x, axis, step, size):
    return lax.ppermute(x, axis, [(i, (i + step) % size) for i in range(size)])


def shift_y(x, step):
    at = [y % 2 * 2 + y // 2 for y in range(4)]
    return lax.ppermute(x, ("yl", "yh"), [(at[y], at[(y + step) % 4]) for y in range(4)])


def pick_kernel(rows, offsets, factors, mine, other, sem):
    c = lax.axis_index("c")
    first = pltpu.make_async_copy(factors.at[offsets[c] % rows], mine, sem.at[0])
    second = pltpu.make_async_copy(factors.at[offsets[1 - c] % rows], other, sem.at[1])
    first.start()
    second.start()
    first.wait()
    second.wait()


def halve_kernel(rows, offsets, mine, swapped, keep, send, sem):
    c, h = lax.axis_index("c"), lax.axis_index("yh")
    size = keep.shape[0]

    def move(source):
        first = pltpu.make_async_copy(source.at[pl.ds(h * size, size), :], keep, sem.at[0])
        second = pltpu.make_async_copy(source.at[pl.ds((1 - h) * size, size), :], send, sem.at[1])
        first.start()
        second.start()
        first.wait()
        second.wait()

    here = offsets[c] // rows % 2 == c

    @pl.when(here)
    def _():
        move(mine)

    @pl.when(jnp.logical_not(here))
    def _():
        move(swapped)


def choose_kernel(rows, offsets, keep, got, out, sem):
    here = offsets[lax.axis_index("c")] // (2 * rows) % 2 == lax.axis_index("yh")
    for source, wanted in ((keep, here), (got, jnp.logical_not(here))):
        @pl.when(wanted)
        def _():
            copy = pltpu.make_async_copy(source, out, sem.at[0])
            copy.start()
            copy.wait()


def choose_z_kernel(rows, offsets, own, up, down, far, out, sem):
    rel = (offsets[lax.axis_index("c")] // (4 * rows) + 4 - lax.axis_index("z")) % 4
    for source, wanted in ((own, 0), (down, 1), (far, 2), (up, 3)):
        @pl.when(rel == wanted)
        def _():
            copy = pltpu.make_async_copy(source, out, sem.at[0])
            copy.start()
            copy.wait()


def lay_kernel(first, second, out):
    count, depth, width = first.shape
    wide = depth // DB * LANES
    for half, piece in enumerate((first, second)):
        for i in range(count):
            row = (half * count + i) * DB
            for d in range(depth // DB):
                block = piece[i, d * DB:(d + 1) * DB, :]
                for n in range(width // LANES):
                    at = n * wide + d * LANES
                    out[row:row + DB, at:at + LANES] = block[:, n * LANES:(n + 1) * LANES]


def lay(first, second):
    count, depth, width = first.shape
    return pl.pallas_call(
        lay_kernel,
        out_shape=jax.ShapeDtypeStruct((2 * count * DB, depth // DB * width), jnp.bfloat16),
        in_specs=[IN_VMEM] * 2,
        out_specs=IN_VMEM,
        compiler_params=pltpu.CompilerParams(vmem_limit_bytes=4 << 20),
        cost_estimate=pl.CostEstimate(flops=0, bytes_accessed=2 << 20, transcendentals=0),
        name="lay",
    )(first, second)


def take_kernel(source, out, sem):
    copy = pltpu.make_async_copy(source.at[pl.ds(0, out.shape[0]), :], out, sem.at[0])
    copy.start()
    copy.wait()


def hold_kernel(source, out, sem):
    copy = pltpu.make_async_copy(source, out, sem.at[0])
    copy.start()
    copy.wait()


def hold(factors):
    return pl.pallas_call(
        hold_kernel,
        out_shape=jax.ShapeDtypeStruct(factors.shape, factors.dtype),
        in_specs=[IN_HBM],
        out_specs=IN_VMEM,
        scratch_shapes=[pltpu.SemaphoreType.DMA((1,))],
        compiler_params=pltpu.CompilerParams(vmem_limit_bytes=1 << 20),
        cost_estimate=pl.CostEstimate(flops=0, bytes_accessed=16 << 20, transcendentals=0),
        name="hold",
    )(factors)


def place_kernel(own, up, down, far, out, sem):
    y = lax.axis_index("yh") * 2 + lax.axis_index("yl")
    size = own.shape[0]
    copies = []
    for n, (piece, step) in enumerate(((own, 0), (up, 3), (down, 1), (far, 2))):
        at = (y + step) % 4
        at = at % 2 * 2 + at // 2
        copies.append(pltpu.make_async_copy(piece, out.at[pl.ds(at * size, size), :], sem.at[n]))
    for copy in copies:
        copy.start()
    for copy in copies:
        copy.wait()


ANY = pl.BlockSpec(memory_space=pl.ANY)
SMALL = pl.BlockSpec(memory_space=pltpu.SMEM)


def move_call(body, name, shapes, n_in, n_sem, small=True):
    specs = ([SMALL] if small else []) + [ANY] * n_in
    return pl.pallas_call(
        body,
        out_shape=[jax.ShapeDtypeStruct(shape, jnp.bfloat16) for shape in shapes],
        in_specs=specs,
        out_specs=[ANY] * len(shapes),
        scratch_shapes=[pltpu.SemaphoreType.DMA((n_sem,))],
        compiler_params=pltpu.CompilerParams(vmem_limit_bytes=1 << 20),
        cost_estimate=pl.CostEstimate(flops=0, bytes_accessed=1 << 20, transcendentals=0),
        name=name,
    )


def integrals(held, pieces, flips, out):
    rows, cols, aux = held.shape
    deep = 2 * DB
    side = [p[...] for p in pieces]
    side = jnp.concatenate(side, axis=0)
    for step in range(cols // deep):
        yield step
        slab = held[:, step * deep:(step + 1) * deep, :].reshape(rows * deep, aux)
        value = lax.dot_general(slab, side, (((1,), (1,)), ((), ())), preferred_element_type=jnp.float32)
        value = value.astype(jnp.bfloat16).reshape(rows, deep // DB, DB, side.shape[0])
        for n in range(side.shape[0] // LANES):
            k = (n + flips[n // 2]) % 2
            for d in range(deep // DB):
                block = value[:, d, :, n * LANES:(n + 1) * LANES].reshape(rows * DB, LANES)
                at = step * deep // DB + d
                out[n // 2, k * rows * DB:(k + 1) * rows * DB, at * LANES:(at + 1) * LANES] = block


def first_kernel(factors, first, second, out, held, sem):
    deep = 2 * DB
    copies = []
    for step in range(held.shape[1] // deep):
        part = pl.ds(step * deep, deep)
        copies.append(pltpu.make_async_copy(factors.at[:, part, :], held.at[:, part, :], sem.at[step]))
        copies[-1].start()
    for step in integrals(held, (first, second), (0,), out):
        copies[step].wait()


def next_kernel(flips, held, *refs):
    for _ in integrals(held, refs[:-1], flips, refs[-1]):
        pass


IN_VMEM = pl.BlockSpec(memory_space=pltpu.VMEM)
IN_HBM = pl.BlockSpec(memory_space=pltpu.HBM)


def integrals_of(factors, pieces, flips, name, load=False):
    rows, cols, aux = factors.shape
    count = len(flips)
    out_shape = [jax.ShapeDtypeStruct((count, 2 * rows * DB, cols // DB * LANES), jnp.bfloat16)]
    if load:
        out_shape.append(jax.ShapeDtypeStruct(factors.shape, factors.dtype))
    return pl.pallas_call(
        first_kernel if load else functools.partial(next_kernel, flips),
        out_shape=out_shape,
        in_specs=[IN_HBM if load else IN_VMEM] + [IN_VMEM] * len(pieces),
        out_specs=[IN_VMEM] * len(out_shape),
        scratch_shapes=[pltpu.SemaphoreType.DMA((4,))] if load else [],
        compiler_params=pltpu.CompilerParams(vmem_limit_bytes=12 << 20),
        cost_estimate=pl.CostEstimate(flops=2 * 256 * count * 2048 * 2048, bytes_accessed=10 << 20, transcendentals=0),
        name=name,
    )(factors, *pieces)


def products(ints, chunks, pieces):
    x, c = lax.axis_index("x"), lax.axis_index("c")
    wide = ints[0].shape[2]
    ahead = jnp.where(c == 0, 3, 1)
    chunk = (x, (x + ahead) % 4, (x + 4 - ahead) % 4, (x + 2) % 4)
    where_int = [(i, n) for i in ints for n in range(i.shape[0])]
    total = None
    for (ref, inner), at in zip(where_int, chunks):
        at = pl.ds(pl.multiple_of(chunk[at] * wide, wide), wide)
        side = jnp.concatenate([p[:, at] for p in pieces], axis=0)
        value = lax.dot_general(ref[inner], side, (((1,), (1,)), ((), ())), preferred_element_type=jnp.float32)
        total = value if total is None else total + value
    return total


def early_kernel(*refs):
    ints, pieces, out = refs[:2], refs[2:-1], refs[-1]
    for g in range(out.shape[0]):
        total = products(ints, (0, 1, 2), pieces[2 * g:2 * g + 2])
        for n in range(total.shape[1] // LANES):
            out[g, n] = total[:, n * LANES:(n + 1) * LANES]


def late_kernel(*refs):
    ints, pieces, before, out, spare = refs[:3], refs[3:-3], refs[-3], refs[-2], refs[-1]
    z, h, c = (lax.axis_index(a) for a in ("z", "yh", "c"))
    ahead = jnp.where(c == 0, 3, 1)
    here = (c, 1 - c)
    away = (1 - c, c)
    places = (
        (z, h, here), (z, 1 - h, here),
        ((z + ahead) % 4, h, here), ((z + 4 - ahead) % 4, h, away),
        ((z + ahead) % 4, 1 - h, here), ((z + 4 - ahead) % 4, 1 - h, away),
        ((z + 2) % 4, h, here), ((z + 2) % 4, 1 - h, here),
    )
    groups, parts, rows, _ = before.shape
    depth = parts * LANES
    for g in range(groups + 1):
        if g < groups:
            total = products(ints[2:], (3,), pieces[2 * g:2 * g + 2])
        else:
            total = products(ints, (0, 1, 2, 3), pieces[2 * groups:])
        for n in range(parts):
            value = total[:, n * LANES:(n + 1) * LANES]
            spare[g, n] = value + before[g, n] if g < groups else value
    small = rows // DB
    folds = depth // DB
    fold = (lax.broadcasted_iota(jnp.int32, (folds, depth), 1) // DB
            == lax.broadcasted_iota(jnp.int32, (folds, depth), 0)).astype(jnp.float32)
    lane = lax.broadcasted_iota(jnp.int32, (small, LANES), 1) % DB
    for g in range(groups + 1):
        columns = []
        for n in range(parts):
            source = spare.at[g, n]
            total = source[pl.ds(0, small, stride=DB), :]
            for d in range(1, DB):
                total = jnp.where(lane == d, source[pl.ds(d, small, stride=DB), :], total)
            columns.append(total)
        total = jnp.concatenate(columns, axis=1)
        total = jnp.where(c == 0, total, jnp.concatenate([total[small // 2:], total[:small // 2]], axis=0))
        total = lax.dot_general(fold, total, (((1,), (1,)), ((), ())),
                                precision=lax.Precision.HIGHEST, preferred_element_type=jnp.float32)
        total = total.reshape(4, folds // 4, small)
        for n in range(4):
            at_z, at_h, cores = places[2 * g + n // 2]
            out[at_z * 4 + at_h * 2 + cores[n % 2]] = total[n]


def contract(ints, pieces, before):
    rows, depth = ints[0].shape[1], 256
    groups = sum(p.shape[0] for p in pieces) // depth
    kept = jax.ShapeDtypeStruct((groups, depth // LANES, rows, LANES), jnp.float32)
    if before is None:
        out_shape = kept
    else:
        out_shape = jax.ShapeDtypeStruct((16, 8, rows // DB), jnp.float32)
    given = list(ints) + list(pieces) + ([] if before is None else [before])
    return pl.pallas_call(
        early_kernel if before is None else late_kernel,
        out_shape=out_shape,
        in_specs=[IN_VMEM] * len(given),
        out_specs=IN_VMEM,
        scratch_shapes=[] if before is None else [pltpu.VMEM(kept.shape, kept.dtype)],
        compiler_params=pltpu.CompilerParams(vmem_limit_bytes=12 << 20),
        cost_estimate=pl.CostEstimate(
            flops=2 * rows * depth * 1024 * (9 if before is None else 7), bytes_accessed=8 << 20, transcendentals=0),
        name="contract_early" if before is None else "contract_late",
    )(*given)


def finish_kernel(pairs, offsets, occupied, virtual, parts, energies, residual, update):
    count, width = parts.shape
    total = parts[...].reshape(16, count // 16, width).sum(axis=1)
    wide = width // 2
    occupied_sum = occupied[pairs[0, 0]] + occupied[pairs[0, 1]]
    every = energies[...].reshape(1, energies.shape[0])
    for k in range(2):
        row = jnp.concatenate([total[n:n + 1, k * wide:(k + 1) * wide] for n in range(16)], axis=1)
        residual[0, k:k + 1, :] = row
        update[0, k:k + 1, :] = row / (virtual[offsets[k]] + every - occupied_sum)


def core_swap(x):
    return shift(x, "c", 1, 2)


def both_ways(x, axis):
    pairs = [(i * 2 + c, (i + (1 if c == 0 else 3)) % 4 * 2 + c) for i in range(4) for c in range(2)]
    return lax.ppermute(x, (axis, "c"), pairs)


def local(amplitudes, factors, pair_list, window_offsets, occupied_energy, virtual_energy):
    rows_here, cols_here, aux = factors.shape
    virt = amplitudes.shape[1]
    n_d = cols_here // DB
    c = lax.axis_index("c")
    factors = pltpu.with_memory_space_constraint(factors, pltpu.HBM)

    tau = amplitudes[0].T.reshape(8, cols_here, virt)
    tau = lax.all_to_all(tau, PAIR, split_axis=0, concat_axis=0, tiled=True)
    mine, other = move_call(
        functools.partial(pick_kernel, rows_here), "pick", [(cols_here, aux)] * 2, 1, 2)(window_offsets, factors)
    swapped = core_swap(other)
    keep, send = move_call(
        functools.partial(halve_kernel, rows_here), "halve", [(cols_here // 2, aux)] * 2, 2, 2)(
            window_offsets, mine, swapped)

    got = shift(send, "yh", 1, 2)
    arow, = move_call(
        functools.partial(choose_kernel, rows_here), "choose", [(cols_here // 2, aux)], 2, 1)(window_offsets, keep, got)
    arow, tau = lax.optimization_barrier((arow, tau))
    tau_h = shift(tau, "yh", 1, 2)
    tau = lay(tau, core_swap(tau))
    arow, factors = lax.optimization_barrier((arow, factors))
    held = hold(factors)
    up, down, far = (shift(arow, "z", s, 4) for s in (1, -1, 2))
    arow, = move_call(
        functools.partial(choose_z_kernel, rows_here), "choose_z", [(cols_here // 2, aux)], 4, 1)(
            window_offsets, arow, up, down, far)
    arow, tau, tau_h, held = lax.optimization_barrier((arow, tau, tau_h, held))

    side_tau = both_ways(tau, "z")
    tau_h = lay(tau_h, core_swap(tau_h))
    side_h = both_ways(tau_h, "z")
    up, down, far = (shift_y(arow, s) for s in (1, -1, 2))
    near, = move_call(place_kernel, "place", [(2 * cols_here, aux)], 4, 4, False)(arow, up, down, far)
    near, tau_h = lax.optimization_barrier((near, tau_h))

    near_c = core_swap(near)
    side = both_ways(near, "x")
    side_c = both_ways(near_c, "x")
    take = move_call(take_kernel, "take", [(tau.shape[0] // 2, tau.shape[1])], 1, 1, False)
    far_tau = both_ways(take(side_tau)[0], "z")
    held, side_tau, side_h = lax.optimization_barrier((held, side_tau, side_h))
    far_h = both_ways(take(side_h)[0], "z")
    ints_near, = integrals_of(held, [near, near_c], (0,), "integrals_near")
    side, side_c, ints_near, far_tau = lax.optimization_barrier((side, side_c, ints_near, far_tau))
    far = both_ways(side, "x")
    ints_side, = integrals_of(
        held, [side, side_c, core_swap(side), core_swap(side_c)], (0, 1), "integrals_side")
    pieces = [tau, tau_h, side_tau, core_swap(side_tau), side_h, core_swap(side_h)]
    partial = contract([ints_near, ints_side], pieces, None)
    far, partial = lax.optimization_barrier((far, partial))
    ints_far, = integrals_of(held, [far, core_swap(far)], (0,), "integrals_far")
    pieces += [far_tau, core_swap(far_tau), far_h, core_swap(far_h)]
    partial = contract([ints_near, ints_side, ints_far], pieces, partial)

    parts = lax.all_to_all(partial.reshape(128, 2 * rows_here), TILE + PAIR, split_axis=0, concat_axis=0, tiled=True)
    residual, update = pl.pallas_call(
        finish_kernel,
        out_shape=[jax.ShapeDtypeStruct((1, 2, 16 * rows_here), jnp.float32)] * 2,
        in_specs=[SMALL] * 4 + [IN_VMEM] * 2,
        out_specs=[IN_VMEM] * 2,
        compiler_params=pltpu.CompilerParams(vmem_limit_bytes=1 << 20),
        name="finish",
    )(pair_list, window_offsets, occupied_energy, virtual_energy, parts, virtual_energy)
    return residual, update


def solution(mesh):
    fine = Mesh(mesh.devices.reshape(4, 2, 4, 2, 2), PAIR + TILE)
    return jax.shard_map(
        local,
        mesh=fine,
        in_specs=(P(PAIR + TILE, None, None), P(TILE, PAIR, None), P(PAIR + TILE, None), P(), P(), P()),
        out_specs=(P(PAIR + TILE, None, None), P(PAIR + TILE, None, None)),
        check_vma=False,
    )
```

```python
import functools

import jax
import jax.numpy as jnp
from jax import lax
from jax.experimental import pallas as pl
from jax.experimental.pallas import tpu as pltpu
from jax.sharding import Mesh, PartitionSpec as P

PAIR = ("x", "yl")
TILE = ("z", "yh", "c")
DB = 8
LANES = 128


def shift(x, axis, step, size):
    return lax.ppermute(x, axis, [(i, (i + step) % size) for i in range(size)])


def shift_y(x, step):
    at = [y % 2 * 2 + y // 2 for y in range(4)]
    return lax.ppermute(x, ("yl", "yh"), [(at[y], at[(y + step) % 4]) for y in range(4)])


def pick_kernel(rows, offsets, factors, mine, other, sem):
    c = lax.axis_index("c")
    first = pltpu.make_async_copy(factors.at[offsets[c] % rows], mine, sem.at[0])
    second = pltpu.make_async_copy(factors.at[offsets[1 - c] % rows], other, sem.at[1])
    first.start()
    second.start()
    first.wait()
    second.wait()


def halve_kernel(rows, offsets, mine, swapped, keep, send, sem):
    c, h = lax.axis_index("c"), lax.axis_index("yh")
    size = keep.shape[0]

    def move(source):
        first = pltpu.make_async_copy(source.at[pl.ds(h * size, size), :], keep, sem.at[0])
        second = pltpu.make_async_copy(source.at[pl.ds((1 - h) * size, size), :], send, sem.at[1])
        first.start()
        second.start()
        first.wait()
        second.wait()

    here = offsets[c] // rows % 2 == c

    @pl.when(here)
    def _():
        move(mine)

    @pl.when(jnp.logical_not(here))
    def _():
        move(swapped)


def choose_kernel(rows, offsets, keep, got, out, sem):
    here = offsets[lax.axis_index("c")] // (2 * rows) % 2 == lax.axis_index("yh")
    for source, wanted in ((keep, here), (got, jnp.logical_not(here))):
        @pl.when(wanted)
        def _():
            copy = pltpu.make_async_copy(source, out, sem.at[0])
            copy.start()
            copy.wait()


def choose_z_kernel(rows, offsets, own, up, down, far, out, sem):
    rel = (offsets[lax.axis_index("c")] // (4 * rows) + 4 - lax.axis_index("z")) % 4
    for source, wanted in ((own, 0), (down, 1), (far, 2), (up, 3)):
        @pl.when(rel == wanted)
        def _():
            copy = pltpu.make_async_copy(source, out, sem.at[0])
            copy.start()
            copy.wait()


def lay_kernel(first, second, out):
    count, depth, width = first.shape
    wide = depth // DB * LANES
    for half, piece in enumerate((first, second)):
        for i in range(count):
            row = (half * count + i) * DB
            for d in range(depth // DB):
                block = piece[i, d * DB:(d + 1) * DB, :]
                for n in range(width // LANES):
                    at = n * wide + d * LANES
                    out[row:row + DB, at:at + LANES] = block[:, n * LANES:(n + 1) * LANES]


def lay(first, second):
    count, depth, width = first.shape
    return pl.pallas_call(
        lay_kernel,
        out_shape=jax.ShapeDtypeStruct((2 * count * DB, depth // DB * width), jnp.bfloat16),
        in_specs=[IN_VMEM] * 2,
        out_specs=IN_VMEM,
        compiler_params=pltpu.CompilerParams(vmem_limit_bytes=4 << 20),
        cost_estimate=pl.CostEstimate(flops=0, bytes_accessed=2 << 20, transcendentals=0),
        name="lay",
    )(first, second)


def take_kernel(source, out, sem):
    copy = pltpu.make_async_copy(source.at[pl.ds(0, out.shape[0]), :], out, sem.at[0])
    copy.start()
    copy.wait()


def hold_kernel(source, out, sem):
    copy = pltpu.make_async_copy(source, out, sem.at[0])
    copy.start()
    copy.wait()


def hold(factors):
    return pl.pallas_call(
        hold_kernel,
        out_shape=jax.ShapeDtypeStruct(factors.shape, factors.dtype),
        in_specs=[IN_HBM],
        out_specs=IN_VMEM,
        scratch_shapes=[pltpu.SemaphoreType.DMA((1,))],
        compiler_params=pltpu.CompilerParams(vmem_limit_bytes=1 << 20),
        cost_estimate=pl.CostEstimate(flops=0, bytes_accessed=16 << 20, transcendentals=0),
        name="hold",
    )(factors)


def place_kernel(own, up, down, far, out, sem):
    y = lax.axis_index("yh") * 2 + lax.axis_index("yl")
    size = own.shape[0]
    copies = []
    for n, (piece, step) in enumerate(((own, 0), (up, 3), (down, 1), (far, 2))):
        at = (y + step) % 4
        at = at % 2 * 2 + at // 2
        copies.append(pltpu.make_async_copy(piece, out.at[pl.ds(at * size, size), :], sem.at[n]))
    for copy in copies:
        copy.start()
    for copy in copies:
        copy.wait()


ANY = pl.BlockSpec(memory_space=pl.ANY)
SMALL = pl.BlockSpec(memory_space=pltpu.SMEM)


def move_call(body, name, shapes, n_in, n_sem, small=True):
    specs = ([SMALL] if small else []) + [ANY] * n_in
    return pl.pallas_call(
        body,
        out_shape=[jax.ShapeDtypeStruct(shape, jnp.bfloat16) for shape in shapes],
        in_specs=specs,
        out_specs=[ANY] * len(shapes),
        scratch_shapes=[pltpu.SemaphoreType.DMA((n_sem,))],
        compiler_params=pltpu.CompilerParams(vmem_limit_bytes=1 << 20),
        cost_estimate=pl.CostEstimate(flops=0, bytes_accessed=1 << 20, transcendentals=0),
        name=name,
    )


def integrals(held, pieces, flips, out):
    rows, cols, aux = held.shape
    deep = 2 * DB
    side = [p[...] for p in pieces]
    side = jnp.concatenate(side, axis=0)
    for step in range(cols // deep):
        yield step
        slab = held[:, step * deep:(step + 1) * deep, :].reshape(rows * deep, aux)
        value = lax.dot_general(slab, side, (((1,), (1,)), ((), ())), preferred_element_type=jnp.float32)
        value = value.astype(jnp.bfloat16).reshape(rows, deep // DB, DB, side.shape[0])
        for n in range(side.shape[0] // LANES):
            k = (n + flips[n // 2]) % 2
            for d in range(deep // DB):
                block = value[:, d, :, n * LANES:(n + 1) * LANES].reshape(rows * DB, LANES)
                at = step * deep // DB + d
                out[n // 2, k * rows * DB:(k + 1) * rows * DB, at * LANES:(at + 1) * LANES] = block


def first_kernel(factors, first, second, out, held, sem):
    deep = 2 * DB
    copies = []
    for step in range(held.shape[1] // deep):
        part = pl.ds(step * deep, deep)
        copies.append(pltpu.make_async_copy(factors.at[:, part, :], held.at[:, part, :], sem.at[step]))
        copies[-1].start()
    for step in integrals(held, (first, second), (0,), out):
        copies[step].wait()


def next_kernel(flips, held, *refs):
    for _ in integrals(held, refs[:-1], flips, refs[-1]):
        pass


IN_VMEM = pl.BlockSpec(memory_space=pltpu.VMEM)
IN_HBM = pl.BlockSpec(memory_space=pltpu.HBM)


def integrals_of(factors, pieces, flips, name, load=False):
    rows, cols, aux = factors.shape
    count = len(flips)
    out_shape = [jax.ShapeDtypeStruct((count, 2 * rows * DB, cols // DB * LANES), jnp.bfloat16)]
    if load:
        out_shape.append(jax.ShapeDtypeStruct(factors.shape, factors.dtype))
    return pl.pallas_call(
        first_kernel if load else functools.partial(next_kernel, flips),
        out_shape=out_shape,
        in_specs=[IN_HBM if load else IN_VMEM] + [IN_VMEM] * len(pieces),
        out_specs=[IN_VMEM] * len(out_shape),
        scratch_shapes=[pltpu.SemaphoreType.DMA((4,))] if load else [],
        compiler_params=pltpu.CompilerParams(vmem_limit_bytes=12 << 20),
        cost_estimate=pl.CostEstimate(flops=2 * 256 * count * 2048 * 2048, bytes_accessed=10 << 20, transcendentals=0),
        name=name,
    )(factors, *pieces)


def products(ints, chunks, pieces):
    x, c = lax.axis_index("x"), lax.axis_index("c")
    wide = ints[0].shape[2]
    ahead = jnp.where(c == 0, 3, 1)
    chunk = (x, (x + ahead) % 4, (x + 4 - ahead) % 4, (x + 2) % 4)
    where_int = [(i, n) for i in ints for n in range(i.shape[0])]
    total = None
    for (ref, inner), at in zip(where_int, chunks):
        at = pl.ds(pl.multiple_of(chunk[at] * wide, wide), wide)
        side = jnp.concatenate([p[:, at] for p in pieces], axis=0)
        value = lax.dot_general(ref[inner], side, (((1,), (1,)), ((), ())), preferred_element_type=jnp.float32)
        total = value if total is None else total + value
    return total


def early_kernel(*refs):
    ints, pieces, out = refs[:2], refs[2:-1], refs[-1]
    for g in range(out.shape[0]):
        total = products(ints, (0, 1, 2), pieces[2 * g:2 * g + 2])
        for n in range(total.shape[1] // LANES):
            out[g, n] = total[:, n * LANES:(n + 1) * LANES]


def late_kernel(*refs):
    ints, pieces, before, out, spare = refs[:3], refs[3:-3], refs[-3], refs[-2], refs[-1]
    z, h, c = (lax.axis_index(a) for a in ("z", "yh", "c"))
    ahead = jnp.where(c == 0, 3, 1)
    here = (c, 1 - c)
    away = (1 - c, c)
    places = (
        (z, h, here), (z, 1 - h, here),
        ((z + ahead) % 4, h, here), ((z + 4 - ahead) % 4, h, away),
        ((z + ahead) % 4, 1 - h, here), ((z + 4 - ahead) % 4, 1 - h, away),
        ((z + 2) % 4, h, here), ((z + 2) % 4, 1 - h, here),
    )
    groups, parts, rows, _ = before.shape
    depth = parts * LANES
    for g in range(groups + 1):
        if g < groups:
            total = products(ints[2:], (3,), pieces[2 * g:2 * g + 2])
        else:
            total = products(ints, (0, 1, 2, 3), pieces[2 * groups:])
        for n in range(parts):
            value = total[:, n * LANES:(n + 1) * LANES]
            spare[g, n] = value + before[g, n] if g < groups else value
    small = rows // DB
    folds = depth // DB
    fold = (lax.broadcasted_iota(jnp.int32, (folds, depth), 1) // DB
            == lax.broadcasted_iota(jnp.int32, (folds, depth), 0)).astype(jnp.float32)
    lane = lax.broadcasted_iota(jnp.int32, (small, LANES), 1) % DB
    for g in range(groups + 1):
        columns = []
        for n in range(parts):
            source = spare.at[g, n]
            total = source[pl.ds(0, small, stride=DB), :]
            for d in range(1, DB):
                total = jnp.where(lane == d, source[pl.ds(d, small, stride=DB), :], total)
            columns.append(total)
        total = jnp.concatenate(columns, axis=1)
        total = jnp.where(c == 0, total, jnp.concatenate([total[small // 2:], total[:small // 2]], axis=0))
        total = lax.dot_general(fold, total, (((1,), (1,)), ((), ())),
                                precision=lax.Precision.HIGHEST, preferred_element_type=jnp.float32)
        total = total.reshape(4, folds // 4, small)
        for n in range(4):
            at_z, at_h, cores = places[2 * g + n // 2]
            out[at_z * 4 + at_h * 2 + cores[n % 2]] = total[n]


def contract(ints, pieces, before):
    rows, depth = ints[0].shape[1], 256
    groups = sum(p.shape[0] for p in pieces) // depth
    kept = jax.ShapeDtypeStruct((groups, depth // LANES, rows, LANES), jnp.float32)
    if before is None:
        out_shape = kept
    else:
        out_shape = jax.ShapeDtypeStruct((16, 8, rows // DB), jnp.float32)
    given = list(ints) + list(pieces) + ([] if before is None else [before])
    return pl.pallas_call(
        early_kernel if before is None else late_kernel,
        out_shape=out_shape,
        in_specs=[IN_VMEM] * len(given),
        out_specs=IN_VMEM,
        scratch_shapes=[] if before is None else [pltpu.VMEM(kept.shape, kept.dtype)],
        compiler_params=pltpu.CompilerParams(vmem_limit_bytes=12 << 20),
        cost_estimate=pl.CostEstimate(
            flops=2 * rows * depth * 1024 * (9 if before is None else 7), bytes_accessed=8 << 20, transcendentals=0),
        name="contract_early" if before is None else "contract_late",
    )(*given)


def finish_kernel(pairs, offsets, occupied, virtual, parts, energies, residual, update):
    count, width = parts.shape
    total = parts[...].reshape(16, count // 16, width).sum(axis=1)
    wide = width // 2
    occupied_sum = occupied[pairs[0, 0]] + occupied[pairs[0, 1]]
    every = energies[...].reshape(1, energies.shape[0])
    for k in range(2):
        row = jnp.concatenate([total[n:n + 1, k * wide:(k + 1) * wide] for n in range(16)], axis=1)
        residual[0, k:k + 1, :] = row
        update[0, k:k + 1, :] = row / (virtual[offsets[k]] + every - occupied_sum)


def core_swap(x):
    return shift(x, "c", 1, 2)


def both_ways(x, axis):
    pairs = [(i * 2 + c, (i + (1 if c == 0 else 3)) % 4 * 2 + c) for i in range(4) for c in range(2)]
    return lax.ppermute(x, (axis, "c"), pairs)


def local(amplitudes, factors, pair_list, window_offsets, occupied_energy, virtual_energy):
    rows_here, cols_here, aux = factors.shape
    virt = amplitudes.shape[1]
    n_d = cols_here // DB
    c = lax.axis_index("c")
    factors = pltpu.with_memory_space_constraint(factors, pltpu.HBM)

    mine, other = move_call(
        functools.partial(pick_kernel, rows_here), "pick", [(cols_here, aux)] * 2, 1, 2)(window_offsets, factors)
    mine, other, amplitudes = lax.optimization_barrier((mine, other, amplitudes))
    swapped = core_swap(other)
    tau = amplitudes[0].T.reshape(8, cols_here, virt)
    tau = lax.all_to_all(tau, PAIR, split_axis=0, concat_axis=0, tiled=True)
    keep, send = move_call(
        functools.partial(halve_kernel, rows_here), "halve", [(cols_here // 2, aux)] * 2, 2, 2)(
            window_offsets, mine, swapped)

    got = shift(send, "yh", 1, 2)
    arow, = move_call(
        functools.partial(choose_kernel, rows_here), "choose", [(cols_here // 2, aux)], 2, 1)(window_offsets, keep, got)
    arow, tau = lax.optimization_barrier((arow, tau))
    tau_h = shift(tau, "yh", 1, 2)
    tau = lay(tau, core_swap(tau))
    arow, factors = lax.optimization_barrier((arow, factors))
    held = hold(factors)
    up, down, far = (shift(arow, "z", s, 4) for s in (1, -1, 2))
    arow, = move_call(
        functools.partial(choose_z_kernel, rows_here), "choose_z", [(cols_here // 2, aux)], 4, 1)(
            window_offsets, arow, up, down, far)
    arow, tau, tau_h, held = lax.optimization_barrier((arow, tau, tau_h, held))

    side_tau = both_ways(tau, "z")
    tau_h = lay(tau_h, core_swap(tau_h))
    side_h = both_ways(tau_h, "z")
    up, down, far = (shift_y(arow, s) for s in (1, -1, 2))
    near, = move_call(place_kernel, "place", [(2 * cols_here, aux)], 4, 4, False)(arow, up, down, far)
    near, tau_h = lax.optimization_barrier((near, tau_h))

    near_c = core_swap(near)
    side = both_ways(near, "x")
    side_c = both_ways(near_c, "x")
    take = move_call(take_kernel, "take", [(tau.shape[0] // 2, tau.shape[1])], 1, 1, False)
    far_tau = both_ways(take(side_tau)[0], "z")
    held, side_tau, side_h = lax.optimization_barrier((held, side_tau, side_h))
    far_h = both_ways(take(side_h)[0], "z")
    ints_near, = integrals_of(held, [near, near_c], (0,), "integrals_near")
    side, side_c, ints_near, far_tau = lax.optimization_barrier((side, side_c, ints_near, far_tau))
    far = both_ways(side, "x")
    ints_side, = integrals_of(
        held, [side, side_c, core_swap(side), core_swap(side_c)], (0, 1), "integrals_side")
    pieces = [tau, tau_h, side_tau, core_swap(side_tau), side_h, core_swap(side_h)]
    partial = contract([ints_near, ints_side], pieces, None)
    far, partial = lax.optimization_barrier((far, partial))
    ints_far, = integrals_of(held, [far, core_swap(far)], (0,), "integrals_far")
    pieces += [far_tau, core_swap(far_tau), far_h, core_swap(far_h)]
    partial = contract([ints_near, ints_side, ints_far], pieces, partial)

    parts = lax.all_to_all(partial.reshape(128, 2 * rows_here), TILE + PAIR, split_axis=0, concat_axis=0, tiled=True)
    residual, update = pl.pallas_call(
        finish_kernel,
        out_shape=[jax.ShapeDtypeStruct((1, 2, 16 * rows_here), jnp.float32)] * 2,
        in_specs=[SMALL] * 4 + [IN_VMEM] * 2,
        out_specs=[IN_VMEM] * 2,
        compiler_params=pltpu.CompilerParams(vmem_limit_bytes=1 << 20),
        name="finish",
    )(pair_list, window_offsets, occupied_energy, virtual_energy, parts, virtual_energy)
    return residual, update


def solution(mesh):
    fine = Mesh(mesh.devices.reshape(4, 2, 4, 2, 2), PAIR + TILE)
    return jax.shard_map(
        local,
        mesh=fine,
        in_specs=(P(PAIR + TILE, None, None), P(TILE, PAIR, None), P(PAIR + TILE, None), P(), P(), P()),
        out_specs=(P(PAIR + TILE, None, None), P(PAIR + TILE, None, None)),
        check_vma=False,
    )
```
